32 devices in a mesh: chan: 8 (over z, x), tm: 4 (over y, core).
Axes of the slice: x: 2, y: 2, z: 4, core: 2. Of those that a mesh axis runs over, the one named last changes fastest.
Arguments:
- raw_traces: bfloat16 [512, 16, 4096], P('chan', 'tm'), may hold values from -6 to 6
- owner_lists: int32 [8, 128], replicated, may hold values from -1 to 511, as said below
- source_owner: int32 [2], replicated, may hold values from 0 to 7
- source_slot: int32 [2, 8], replicated, may hold values from 0 to 31, as said below
Outputs:
- correlations: float32 [1024, 16, 256], P(('chan', 'tm'))
The draws below stay inside these ranges and needn't reach their ends.
Inputs may be any that keep to these rules, and one draw needn't show every extreme that they name: `owner_lists`: row o lists the channels owned by owner o, live entries first and then -1; each of the 512 channels appears exactly once. A quarter of the rows hold 128 live entries, half of them 3 * 16 and a quarter 64 / 2. At most 16 live entries of one row lie in one block of 64 consecutive channels, and some row has exactly 16 in some block. `source_slot`: the 8 entries of a step are distinct and below 32, so they name live channels of that owner.
All inputs are finite; a program needn't handle non-finite values.
Results may differ from the reference program's by a relative error of at most 0.0046.
Values may be sent and summed in bfloat16 or wider, within the bound.
A program may use at most 64 MiB of HBM per device.

```python
import math
import jax
import jax.numpy as jnp
from jax import lax

L1 = 64
L2 = 64
L = 4096
HW = 64
LAGS = 256
NVS = 8
STEPS = 2
C_DEV = 64
OWNERS = 8
C = 512
W = 16
OWN_CAP = 128
N_CHAN = 8


def draw_owner_lists(key, part):
    blocks = C // C_DEV
    key_order, key_place, key_shuffle = jax.random.split(jax.random.fold_in(key, 11), 3)
    pattern = jnp.array([2 * C_DEV, 3 * C_DEV // 4, 3 * C_DEV // 4, C_DEV // 2], dtype=jnp.int32)
    ordered_loads = jnp.tile(pattern, blocks // 4)
    ordered_starts = jnp.cumsum(ordered_loads) - ordered_loads
    owner_order = jax.random.permutation(key_order, blocks)
    loads = jnp.zeros((blocks,), jnp.int32).at[owner_order].set(ordered_loads)
    starts = jnp.zeros((blocks,), jnp.int32).at[owner_order].set(ordered_starts.astype(jnp.int32))
    placing = jax.vmap(lambda sub_key: jax.random.permutation(sub_key, C_DEV))(jax.random.split(key_place, blocks))
    position = jnp.arange(OWN_CAP, dtype=jnp.int32)
    is_live = position[None, :] < loads[:, None]
    scores = jax.random.randint(key_shuffle, (blocks, OWN_CAP), 0, 4096) * OWN_CAP + position[None, :]
    scores = jnp.where(is_live, scores, scores + 4096 * OWN_CAP)
    shuffle = jnp.argsort(scores, axis=1).astype(jnp.int32)
    ticket = jnp.minimum(starts[:, None] + shuffle, C - 1)
    source_block = ticket % blocks
    channel = source_block * C_DEV + placing[source_block, ticket // blocks]
    return jnp.where(is_live, channel, -1).astype(jnp.int32)


def draw_source_slot(key, part):
    half_count = C_DEV // 2
    sub_keys = jax.random.split(jax.random.fold_in(key, 23), STEPS)
    shuffled = jax.vmap(lambda sub_key: jax.random.permutation(sub_key, half_count))(sub_keys)
    lead_row = shuffled[0]
    lead_row = jnp.where(lead_row == half_count - 1, lead_row[0], lead_row).at[0].set(half_count - 1)
    shuffled = shuffled.at[0].set(lead_row)
    return shuffled[:, :NVS].astype(jnp.int32)


def block_scale(own_key, extent, pieces, low, high):
    def one(dim, blocks):
        draws = jax.random.uniform(jax.random.fold_in(jax.random.fold_in(own_key, 6), dim), (blocks,), jnp.float32, low / len(pieces), high / len(pieces))
        return jnp.repeat(jnp.exp(draws), extent[dim] // blocks).reshape((-1,) + (1,) * (len(extent) - dim - 1))

    level = one(*pieces[0])
    for cut in pieces[1:]:
        level = level * one(*cut)
    return level


def normal_values(stream_key, shape, deviation, bound, shards=(), held_as=jnp.bfloat16):
    level = block_scale(stream_key, shape, shards, -0.22, 0.18) if shards else 1.0
    entries = jax.random.normal(stream_key, shape, jnp.float32) * deviation * level
    return jnp.minimum(jnp.maximum(entries, -bound), bound).astype(held_as)


def setup_inputs(seed: int = 0) -> dict:
    seeds = jax.random.split(jax.random.key(seed), 5)
    return {
        "raw_traces": normal_values(seeds[0], (C, W, L), 1.0, 6.0, ((0, 8), (1, 4))),
        "owner_lists": draw_owner_lists(jax.random.fold_in(seeds[4], 71), 0),
        "source_owner": jax.random.randint(seeds[2], (STEPS,), 0, OWNERS).astype(jnp.int32),
        "source_slot": draw_source_slot(jax.random.fold_in(seeds[4], 71), 0),
    }


EPSILON = 1e-06
TWO_PI = 2.0 * math.pi

def make_tables():
    sample = jnp.arange(L, dtype=jnp.int32)
    window_taper = 0.5 - 0.5 * jnp.cos(TWO_PI / L * (sample.astype(jnp.float32) + 0.5))
    inner_index = jnp.arange(L2, dtype=jnp.int32)
    first_angle = TWO_PI / L2 * (inner_index[:, None] * inner_index[None, :] % L2).astype(jnp.float32)
    first_table = jnp.concatenate([jnp.cos(first_angle), -jnp.sin(first_angle)], axis=1).astype(jnp.bfloat16)
    outer_index = jnp.arange(L1, dtype=jnp.int32)
    twist_angle = TWO_PI / L * (outer_index[:, None] * inner_index[None, :] % L).astype(jnp.float32)
    twist_cos = jnp.cos(twist_angle)
    twist_sin = jnp.sin(twist_angle)
    half_index = jnp.arange(L1 // 2, dtype=jnp.int32)
    second_angle = TWO_PI / L1 * (outer_index[:, None] * half_index[None, :] % L1).astype(jnp.float32)
    second_cos = jnp.cos(second_angle)
    second_sin = jnp.sin(second_angle)
    second_table = jnp.concatenate([jnp.concatenate([second_cos, -second_sin], axis=1), jnp.concatenate([second_sin, second_cos], axis=1)], axis=0)
    span_bins = 2 * HW
    band_rows = jnp.arange(3 * span_bins, dtype=jnp.int32)
    band_cols = jnp.arange(span_bins, dtype=jnp.int32)
    band = (jnp.abs(band_rows[:, None] - span_bins - band_cols[None, :]) <= HW).astype(jnp.bfloat16)
    bin_index = jnp.arange(L // 2, dtype=jnp.int32)
    counts = (jnp.minimum(bin_index, HW) + jnp.minimum(L // 2 - 1 - bin_index, HW) + 1).astype(jnp.float32)
    lag_index = jnp.arange(LAGS, dtype=jnp.int32) - LAGS // 2
    lag_angle = TWO_PI / L * (bin_index[:, None] * lag_index[None, :] % L).astype(jnp.float32)
    weights = jnp.where(bin_index == 0, 1.0, 2.0).astype(jnp.float32)[:, None]
    inverse_table = jnp.concatenate([weights * jnp.cos(lag_angle), -weights * jnp.sin(lag_angle)], axis=0)
    return (window_taper, first_table, twist_cos, twist_sin, second_table, band, counts, inverse_table)

def whiten_block(row_block, tables):
    window_taper, first_table, twist_cos, twist_sin, second_table, band, counts = tables
    row_total = row_block.shape[0]
    half_bins = L // 2
    tapered = lax.optimization_barrier((row_block.astype(jnp.float32) * window_taper).astype(jnp.bfloat16))
    tapered = tapered.astype(jnp.float32).reshape(row_total, L2, L1)
    section_one = jnp.einsum('nab,ak->nbk', tapered, first_table.astype(jnp.float32), precision=lax.Precision.HIGHEST)
    real_in = section_one[:, :, :L2]
    imag_in = section_one[:, :, L2:]
    turned = jnp.concatenate([real_in * twist_cos + imag_in * twist_sin, imag_in * twist_cos - real_in * twist_sin], axis=1)
    spectrum = jnp.einsum('ntk,tj->njk', turned, second_table, precision=lax.Precision.HIGHEST)
    real_part = spectrum[:, :L1 // 2].reshape(row_total, half_bins)
    imag_part = spectrum[:, L1 // 2:].reshape(row_total, half_bins)
    magnitude = lax.optimization_barrier(jnp.sqrt(real_part * real_part + imag_part * imag_part).astype(jnp.bfloat16))
    magnitude = magnitude.astype(jnp.float32)
    span_bins = 2 * HW
    blocks = magnitude.reshape(row_total, half_bins // span_bins, span_bins)
    padded = jnp.pad(blocks, ((0, 0), (1, 1), (0, 0)))
    joined = jnp.concatenate([padded[:, :-2], padded[:, 1:-1], padded[:, 2:]], axis=2)
    smooth = jnp.einsum('nbi,ij->nbj', joined, band.astype(jnp.float32), precision=lax.Precision.HIGHEST)
    smooth = smooth.reshape(row_total, half_bins) / counts
    denominator = smooth + EPSILON
    return jnp.concatenate([real_part / denominator, imag_part / denominator], axis=1).astype(jnp.bfloat16)

def reference(raw_traces, owner_lists, source_owner, source_slot):
    tables = make_tables()
    forward = tables[:7]
    inverse_table = tables[7]
    half_bins = L // 2
    row_total = C * W
    group_rows = math.gcd(row_total, 256)
    grouped_rows = raw_traces.reshape(row_total // group_rows, group_rows, L)
    spectra = lax.map(lambda row_block: whiten_block(row_block, forward), grouped_rows).reshape(C, W, L)
    norm_scale = 1.0 / math.sqrt(W * half_bins)
    source_ids = owner_lists[source_owner[:, None], source_slot].reshape(-1)
    sources = spectra[source_ids]
    grouped = spectra.reshape(N_CHAN, C_DEV, W, L)

    def per_source(source):
        source_real = source[:, :half_bins].astype(jnp.float32)
        source_imag = source[:, half_bins:].astype(jnp.float32)

        def per_group(group_spectra):
            group_real = group_spectra[:, :, :half_bins].astype(jnp.float32)
            group_imag = group_spectra[:, :, half_bins:].astype(jnp.float32)
            cross_real = lax.optimization_barrier(jnp.sum(group_real * source_real + group_imag * source_imag, axis=1))
            cross_imag = lax.optimization_barrier(jnp.sum(group_imag * source_real - group_real * source_imag, axis=1))
            stacked = jnp.concatenate([cross_real, cross_imag], axis=1)
            return jnp.dot(stacked, inverse_table, precision=lax.Precision.HIGHEST, preferred_element_type=jnp.float32) * norm_scale
        return lax.map(per_group, grouped).reshape(C, LAGS)
    per_channel = lax.map(per_source, sources)
    ordered = jnp.transpose(per_channel, (1, 0, 2))
    flat_lists = owner_lists.reshape(-1)
    is_live = flat_lists >= 0
    picked = ordered[jnp.where(is_live, flat_lists, 0)]
    return jnp.where(is_live[:, None, None], picked, 0.0).astype(jnp.float32)
```

```python
import functools
import math

import jax
import jax.numpy as jnp
import numpy as np
from jax import lax
from jax.experimental import pallas as pl
from jax.experimental.pallas import tpu as pltpu
from jax.sharding import PartitionSpec as P

L = 4096
HALF = L // 2
HW = 64
LAGS = 256
EPSILON = 1e-06
TB = 16
TA = L // TB
KA = HALF // TB


def make_tables():
    a = np.arange(TA, dtype=np.int64)
    taper = 0.5 - 0.5 * np.cos(2 * np.pi / L * (np.arange(L) + 0.5))
    kb = np.arange(TB // 2 + 1, dtype=np.int64)
    twist = 2 * np.pi / L * (kb[:, None] * a[None, :])
    twist_cos, twist_sin = np.cos(twist), np.sin(twist)
    ka = np.arange(KA, dtype=np.int64)
    low = 2 * np.pi / TA * (a[:, None] * ka[None, :] % TA)
    high = 2 * np.pi / TA * (a[:, None] * (TA - 1 - ka)[None, :] % TA)
    top = [np.cos(low), -np.sin(low), np.cos(high), np.sin(high)]
    bottom = [np.sin(low), np.cos(low), np.sin(high), -np.cos(high)]
    second = np.concatenate([np.concatenate(top, 1), np.concatenate(bottom, 1)], 0)
    bins = np.arange(TB)[:, None] + TB * ka[None, :]
    counts = np.minimum(bins, HW) + np.minimum(HALF - 1 - bins, HW) + 1
    lag = np.arange(LAGS, dtype=np.int64) - LAGS // 2
    angle = 2 * np.pi / L * (bins[:, :, None] * lag % L)
    weight = np.where(bins == 0, 1.0, 2.0)[:, :, None]
    inverse = np.stack([weight * np.cos(angle), -weight * np.sin(angle)], 1)
    f32 = np.float32
    return (
        taper.astype(f32)[None, :],
        twist_cos.astype(f32),
        twist_sin.astype(f32),
        second.astype(jnp.bfloat16),
        (1.0 / counts).astype(f32),
        inverse.reshape(L, LAGS).astype(jnp.bfloat16),
    )


def dft4(x0, x1, x2, x3):
    if x0[1] is None:
        s, d = x0[0] + x2[0], x0[0] - x2[0]
        u, v = x1[0] + x3[0], x1[0] - x3[0]
        return (s + u, None), (d, -v), (s - u, None), (d, v)
    sr, si, dr, di = x0[0] + x2[0], x0[1] + x2[1], x0[0] - x2[0], x0[1] - x2[1]
    ur, ui, vr, vi = x1[0] + x3[0], x1[1] + x3[1], x1[0] - x3[0], x1[1] - x3[1]
    return (sr + ur, si + ui), (dr + vi, di - vr), (sr - ur, si - ui), (dr - vi, di + vr)


def turn(value, step):
    c, s = math.cos(2 * math.pi * step / TB), math.sin(2 * math.pi * step / TB)
    re, im = value
    if step == 0:
        return value
    if im is None:
        return re * c, re * (-s)
    return re * c + im * s, im * c - re * s


def dft16_real(x):
    first = [dft4(*[(x[n + 4 * m], None) for m in range(4)]) for n in range(4)]
    out = [None] * 9
    for q in range(3):
        parts = [turn(first[n][q], n * q) for n in range(4)]
        if q == 0:
            r = [p[0] for p in parts]
            out[0] = (r[0] + r[1] + r[2] + r[3], None)
            out[4] = (r[0] - r[2], r[3] - r[1])
            out[8] = ((r[0] + r[2]) - (r[1] + r[3]), None)
        else:
            if parts[0][1] is None:
                parts[0] = (parts[0][0], jnp.zeros_like(parts[0][0]))
            y = dft4(*parts)
            out[q] = y[0]
            out[q + 4] = y[1]
            if q == 1:
                out[3] = (y[3][0], -y[3][1])
            else:
                pass
    parts = [turn(first[n][1], n) for n in range(4)]
    y = dft4(*parts)
    out[7] = (y[2][0], -y[2][1])
    return out


def whiten_kernel(x_ref, taper_ref, cos_ref, sin_ref, second_ref, count_ref, o_ref, turned, spec):
    rows = x_ref.shape[0]
    place = {q: (q - 1) * rows for q in range(1, 9)}
    place[0] = 8 * rows
    group = 16

    @pl.loop(0, rows // group)
    def _(step):
        base = pl.multiple_of(step * group, group)
        for h in range(TA // 128):
            x = []
            for b in range(TB):
                cols = pl.ds(b * TA + h * 128, 128)
                v = x_ref[pl.ds(base, group), cols].astype(jnp.float32) * taper_ref[:, cols]
                x.append(v.astype(jnp.bfloat16).astype(jnp.float32))
            y = dft16_real(x)
            here = pl.ds(h * 128, 128)
            there = pl.ds(TA + h * 128, 128)
            for q in range(TB // 2 + 1):
                re, im = y[q]
                target = pl.ds(pl.multiple_of(base + place[q], group), group)
                if q == 0:
                    out_re, out_im = re, jnp.zeros_like(re)
                else:
                    c, s = cos_ref[pl.ds(q, 1), here], sin_ref[pl.ds(q, 1), here]
                    if im is None:
                        out_re, out_im = re * c, -(re * s)
                    else:
                        out_re, out_im = re * c + im * s, im * c - re * s
                turned[target, here] = out_re.astype(jnp.bfloat16)
                turned[target, there] = out_im.astype(jnp.bfloat16)

    split = 7 * rows
    spec[0:split, :] = jnp.dot(
        turned[0:split, :], second_ref[...], preferred_element_type=jnp.float32
    )
    spec[split:, 0 : 2 * KA] = jnp.dot(
        turned[split:, :], second_ref[:, 0 : 2 * KA], preferred_element_type=jnp.float32
    )

    lane = lax.broadcasted_iota(jnp.int32, (8, KA), 1)

    def ahead(v, d):
        return jnp.where(lane < KA - d, pltpu.roll(v, KA - d, 1), 0.0)

    def behind(v, d):
        return jnp.where(lane >= d, pltpu.roll(v, d, 1), 0.0)

    @pl.loop(0, rows // 16)
    def _(step):
        done = [[], []]
        for half in range(2):
            base = pl.multiple_of(step * 16, 16) + half * 8

            def part(q, imag):
                src, col = (q, 0) if q <= 8 else (TB - q, 2 * KA)
                at = pl.ds(pl.multiple_of(base + place[src], 8), 8)
                return spec[at, pl.ds(col + imag * KA, KA)]

            mags = []
            for q in range(TB):
                re, im = part(q, 0), part(q, 1)
                m = jnp.sqrt(re * re + im * im)
                mags.append(m.astype(jnp.bfloat16).astype(jnp.float32))
            prefix = [mags[0]]
            for q in range(1, TB):
                prefix.append(prefix[-1] + mags[q])
            total = prefix[-1]
            near = total
            for d in (1, 2, 3):
                near = near + ahead(total, d) + behind(total, d)
            suffix = total
            for q in range(TB):
                smooth = near + behind(suffix, 4) + ahead(prefix[q], 4)
                suffix = suffix - mags[q]
                inv = 1.0 / (smooth * count_ref[pl.ds(q, 1), :] + EPSILON)
                done[half].append((part(q, 0) * inv, part(q, 1) * inv))
        at = pl.ds(pl.multiple_of(step * 16, 16), 16)
        for q in range(TB):
            for p in range(2):
                both = jnp.concatenate([done[0][q][p], done[1][q][p]], axis=0)
                o_ref[at, pl.ds(q * 2 * KA + p * KA, KA)] = both.astype(jnp.bfloat16)


def whiten(rows_by_window, tables):
    rows = rows_by_window.shape[0]
    windows = rows_by_window.shape[1] // L
    taper, tcos, tsin, second, rcount, _ = tables
    full = lambda v: pl.BlockSpec(v.shape, lambda w: (0, 0))
    flops = 2 * 9 * rows * windows * 512 * 512
    return pl.pallas_call(
        whiten_kernel,
        grid=(windows,),
        in_specs=[pl.BlockSpec((rows, L), lambda w: (0, w))]
        + [full(v) for v in (taper, tcos, tsin, second, rcount)],
        out_specs=pl.BlockSpec((rows, L), lambda w: (w, 0)),
        out_shape=jax.ShapeDtypeStruct((windows * rows, L), jnp.bfloat16),
        scratch_shapes=[
            pltpu.VMEM((9 * rows, 2 * TA), jnp.bfloat16),
            pltpu.VMEM((9 * rows, 4 * KA), jnp.float32),
        ],
        cost_estimate=pl.CostEstimate(
            flops=flops, bytes_accessed=4 * rows * windows * L, transcendentals=0
        ),
        name="whiten",
    )(rows_by_window, taper, tcos, tsin, second, rcount)


def correlate_kernel(windows, sources, scale, own_ref, src_ref, inv_ref, o_ref, cross):
    chans = own_ref.shape[0] // windows

    @pl.loop(0, TB)
    def _(q):
        col_re = pl.ds(pl.multiple_of(q * 2 * KA, KA), KA)
        col_im = pl.ds(pl.multiple_of(q * 2 * KA + KA, KA), KA)
        for n in range(sources):
            s_re = [
                jnp.broadcast_to(src_ref[pl.ds(w * sources + n, 1), col_re], (16, KA)).astype(jnp.float32)
                for w in range(windows)
            ]
            s_im = [
                jnp.broadcast_to(src_ref[pl.ds(w * sources + n, 1), col_im], (16, KA)).astype(jnp.float32)
                for w in range(windows)
            ]
            for g in range(chans // 16):
                re = im = None
                for w in range(windows):
                    at = pl.ds(w * chans + g * 16, 16)
                    a = own_ref[at, col_re].astype(jnp.float32)
                    b = own_ref[at, col_im].astype(jnp.float32)
                    r = a * s_re[w] + b * s_im[w]
                    i = b * s_re[w] - a * s_im[w]
                    re = r if re is None else re + r
                    im = i if im is None else im + i
                at = pl.ds(n * chans + g * 16, 16)
                cross[at, col_re] = re.astype(jnp.bfloat16)
                cross[at, col_im] = im.astype(jnp.bfloat16)

    tile = math.gcd(sources * chans, 256)

    @pl.loop(0, sources * chans // tile)
    def _(step):
        at = pl.ds(pl.multiple_of(step * tile, tile), tile)
        out = jnp.dot(cross[at, :], inv_ref[...], preferred_element_type=jnp.float32)
        o_ref[at, :] = (out * scale).astype(jnp.bfloat16)


def correlate(own, src, windows, scale, tables):
    chans, sources = own.shape[0] // windows, src.shape[0] // windows
    inverse = tables[5]
    whole = pl.BlockSpec(memory_space=pltpu.VMEM)
    return pl.pallas_call(
        functools.partial(correlate_kernel, windows, sources, scale),
        in_specs=[whole] * 3,
        out_specs=whole,
        out_shape=jax.ShapeDtypeStruct((sources * chans, LAGS), jnp.bfloat16),
        scratch_shapes=[pltpu.VMEM((sources * chans, L), jnp.bfloat16)],
        name="correlate",
    )(own, src, inverse)


def body(raw_traces, owner_lists, source_owner, source_slot):
    block, windows, length = raw_traces.shape
    owners = lax.axis_size("chan")
    shards = lax.axis_size("tm")
    capacity = owner_lists.shape[1]
    slots = (capacity + owners - 1) // owners
    share = capacity // shards
    me = lax.axis_index("chan")
    tables = tuple(jnp.asarray(t) for t in make_tables())
    scale = 1.0 / math.sqrt(windows * shards * HALF)
    bf16, f32 = jnp.bfloat16, jnp.float32

    traces = raw_traces.reshape(block, windows * length)
    ids = owner_lists[source_owner[:, None], source_slot].reshape(-1)
    sources = ids.shape[0]
    pick = (ids[:, None] == me * block + jnp.arange(block)[None, :]).astype(bf16)
    mine = jnp.dot(pick, traces, preferred_element_type=f32).astype(bf16)
    source_rows = lax.psum(mine, "chan")

    own = whiten(traces, tables)
    src = whiten(source_rows, tables)
    partial = correlate(own, src, windows, scale, tables)

    per = sources // shards
    parts = lax.all_to_all(
        partial.reshape(shards, per, block, LAGS), "tm", split_axis=0, concat_axis=0, tiled=True
    )
    summed = jnp.sum(parts.astype(f32), axis=0).astype(bf16)

    source_block = jnp.floor_divide(owner_lists, block)
    matched = (owner_lists >= 0) & (source_block == me)
    rank = jnp.cumsum(matched.astype(jnp.int32), axis=1) - 1
    slot_ids = jnp.arange(slots, dtype=jnp.int32)
    chosen = matched[:, None, :] & (rank[:, None, :] == slot_ids[None, :, None])
    wanted = jnp.sum(jnp.where(chosen, owner_lists[:, None, :] - me * block + 1, 0), axis=2) - 1
    send = (wanted[:, :, None] == jnp.arange(block)[None, None, :]).astype(bf16)
    outgoing = jnp.einsum("osc,ncl->onsl", send, summed, preferred_element_type=f32).astype(bf16)
    arrived = lax.all_to_all(outgoing, "chan", split_axis=0, concat_axis=0, tiled=True)

    my_list = lax.dynamic_index_in_dim(owner_lists, me, 0, keepdims=False)
    my_block = jnp.floor_divide(my_list, block)
    live = my_list >= 0
    position = jnp.arange(capacity, dtype=jnp.int32)
    same = (my_block[:, None] == my_block[None, :]) & (position[None, :] < position[:, None]) & live[None, :]
    earlier = jnp.sum(same.astype(jnp.int32), axis=1)
    take = (
        live[:, None, None]
        & (my_block[:, None, None] == jnp.arange(owners)[None, :, None])
        & (earlier[:, None, None] == slot_ids[None, None, :])
    ).astype(bf16)
    placed = jnp.einsum("rcs,cnsl->rnl", take, arrived, preferred_element_type=f32).astype(bf16)
    result = lax.all_to_all(placed, "tm", split_axis=0, concat_axis=1, tiled=True)
    return result.astype(f32)


def solution(mesh):
    return jax.shard_map(
        body,
        mesh=mesh,
        in_specs=(P("chan", "tm", None), P(), P(), P()),
        out_specs=P(("chan", "tm"), None, None),
        check_vma=False,
    )
```

```python
import functools
import math

import jax
import jax.numpy as jnp
import numpy as np
from jax import lax
from jax.experimental import pallas as pl
from jax.experimental.pallas import tpu as pltpu
from jax.sharding import PartitionSpec as P

L = 4096
HALF = L // 2
HW = 64
LAGS = 256
EPSILON = 1e-06
TB = 16
TA = L // TB
KA = HALF // TB


def make_tables():
    a = np.arange(TA, dtype=np.int64)
    taper = 0.5 - 0.5 * np.cos(2 * np.pi / L * (np.arange(L) + 0.5))
    kb = np.arange(TB // 2 + 1, dtype=np.int64)
    twist = 2 * np.pi / L * (kb[:, None] * a[None, :])
    twist_cos, twist_sin = np.cos(twist), np.sin(twist)
    ka = np.arange(KA, dtype=np.int64)
    low = 2 * np.pi / TA * (a[:, None] * ka[None, :] % TA)
    high = 2 * np.pi / TA * (a[:, None] * (TA - 1 - ka)[None, :] % TA)
    top = [np.cos(low), -np.sin(low), np.cos(high), np.sin(high)]
    bottom = [np.sin(low), np.cos(low), np.sin(high), -np.cos(high)]
    second = np.concatenate([np.concatenate(top, 1), np.concatenate(bottom, 1)], 0)
    bins = np.arange(TB)[:, None] + TB * ka[None, :]
    counts = np.minimum(bins, HW) + np.minimum(HALF - 1 - bins, HW) + 1
    lag = np.arange(LAGS, dtype=np.int64) - LAGS // 2
    angle = 2 * np.pi / L * (bins[:, :, None] * lag % L)
    weight = np.where(bins == 0, 1.0, 2.0)[:, :, None]
    inverse = np.stack([weight * np.cos(angle), -weight * np.sin(angle)], 1)
    f32 = np.float32
    return (
        taper.astype(f32)[None, :],
        twist_cos.astype(f32),
        twist_sin.astype(f32),
        second.astype(jnp.bfloat16),
        (1.0 / counts).astype(f32),
        inverse.reshape(L, LAGS).astype(jnp.bfloat16),
    )


def dft4(x0, x1, x2, x3):
    if x0[1] is None:
        s, d = x0[0] + x2[0], x0[0] - x2[0]
        u, v = x1[0] + x3[0], x1[0] - x3[0]
        return (s + u, None), (d, -v), (s - u, None), (d, v)
    sr, si, dr, di = x0[0] + x2[0], x0[1] + x2[1], x0[0] - x2[0], x0[1] - x2[1]
    ur, ui, vr, vi = x1[0] + x3[0], x1[1] + x3[1], x1[0] - x3[0], x1[1] - x3[1]
    return (sr + ur, si + ui), (dr + vi, di - vr), (sr - ur, si - ui), (dr - vi, di + vr)


def turn(value, step):
    c, s = math.cos(2 * math.pi * step / TB), math.sin(2 * math.pi * step / TB)
    re, im = value
    if step == 0:
        return value
    if im is None:
        return re * c, re * (-s)
    return re * c + im * s, im * c - re * s


def dft16_real(x):
    first = [dft4(*[(x[n + 4 * m], None) for m in range(4)]) for n in range(4)]
    out = [None] * 9
    for q in range(3):
        parts = [turn(first[n][q], n * q) for n in range(4)]
        if q == 0:
            r = [p[0] for p in parts]
            out[0] = (r[0] + r[1] + r[2] + r[3], None)
            out[4] = (r[0] - r[2], r[3] - r[1])
            out[8] = ((r[0] + r[2]) - (r[1] + r[3]), None)
        else:
            if parts[0][1] is None:
                parts[0] = (parts[0][0], jnp.zeros_like(parts[0][0]))
            y = dft4(*parts)
            out[q] = y[0]
            out[q + 4] = y[1]
            if q == 1:
                out[3] = (y[3][0], -y[3][1])
            else:
                pass
    parts = [turn(first[n][1], n) for n in range(4)]
    y = dft4(*parts)
    out[7] = (y[2][0], -y[2][1])
    return out


def whiten_rows(load, store, tables, turned, spec):
    taper_ref, cos_ref, sin_ref, second_ref, count_ref = tables
    rows = turned.shape[0] // 9
    place = {q: (q - 1) * rows for q in range(1, 9)}
    place[0] = 8 * rows
    group = 16

    @pl.loop(0, rows // group)
    def _(step):
        base = pl.multiple_of(step * group, group)
        for h in range(TA // 128):
            x = []
            for b in range(TB):
                cols = pl.ds(b * TA + h * 128, 128)
                v = load(step, b * TA + h * 128).astype(jnp.float32) * taper_ref[:, cols]
                x.append(v.astype(jnp.bfloat16).astype(jnp.float32))
            y = dft16_real(x)
            here = pl.ds(h * 128, 128)
            there = pl.ds(TA + h * 128, 128)
            for q in range(TB // 2 + 1):
                re, im = y[q]
                target = pl.ds(pl.multiple_of(base + place[q], group), group)
                if q == 0:
                    out_re, out_im = re, jnp.zeros_like(re)
                else:
                    c, s = cos_ref[pl.ds(q, 1), here], sin_ref[pl.ds(q, 1), here]
                    if im is None:
                        out_re, out_im = re * c, -(re * s)
                    else:
                        out_re, out_im = re * c + im * s, im * c - re * s
                turned[target, here] = out_re.astype(jnp.bfloat16)
                turned[target, there] = out_im.astype(jnp.bfloat16)

    split = 7 * rows
    spec[0:split, :] = jnp.dot(
        turned[0:split, :], second_ref[...], preferred_element_type=jnp.float32
    )
    spec[split:, 0 : 2 * KA] = jnp.dot(
        turned[split:, :], second_ref[:, 0 : 2 * KA], preferred_element_type=jnp.float32
    )

    lane = lax.broadcasted_iota(jnp.int32, (8, KA), 1)

    def ahead(v, d):
        return jnp.where(lane < KA - d, pltpu.roll(v, KA - d, 1), 0.0)

    def behind(v, d):
        return jnp.where(lane >= d, pltpu.roll(v, d, 1), 0.0)

    @pl.loop(0, rows // 16)
    def _(step):
        done = [[], []]
        for half in range(2):
            base = pl.multiple_of(step * 16, 16) + half * 8

            def part(q, imag):
                src, col = (q, 0) if q <= 8 else (TB - q, 2 * KA)
                at = pl.ds(pl.multiple_of(base + place[src], 8), 8)
                return spec[at, pl.ds(col + imag * KA, KA)]

            mags = []
            for q in range(TB):
                re, im = part(q, 0), part(q, 1)
                m = jnp.sqrt(re * re + im * im)
                mags.append(m.astype(jnp.bfloat16).astype(jnp.float32))
            prefix = [mags[0]]
            for q in range(1, TB):
                prefix.append(prefix[-1] + mags[q])
            total = prefix[-1]
            near = total
            for d in (1, 2, 3):
                near = near + ahead(total, d) + behind(total, d)
            suffix = total
            for q in range(TB):
                smooth = near + behind(suffix, 4) + ahead(prefix[q], 4)
                suffix = suffix - mags[q]
                inv = 1.0 / (smooth * count_ref[pl.ds(q, 1), :] + EPSILON)
                done[half].append((part(q, 0) * inv, part(q, 1) * inv))
        for q in range(TB):
            for p in range(2):
                both = jnp.concatenate([done[0][q][p], done[1][q][p]], axis=0)
                store(step, q * 2 * KA + p * KA, both.astype(jnp.bfloat16))


def partners(axis, extent):
    me = lax.axis_index(axis)
    return me, [lax.rem(me + k, extent) for k in range(extent)]


def remote(src, dst, send, recv, axis, device):
    return pltpu.make_async_remote_copy(
        src_ref=src,
        dst_ref=dst,
        send_sem=send,
        recv_sem=recv,
        device_id={axis: device},
        device_id_type=pl.DeviceIdType.MESH,
    )


def greet(pairs):
    barrier = pltpu.get_barrier_semaphore()
    for axis, device in pairs:
        pl.semaphore_signal(
            barrier, inc=1, device_id={axis: device}, device_id_type=pl.DeviceIdType.MESH
        )
    pl.semaphore_wait(barrier, len(pairs))


def whiten_kernel(
    owners, windows, traces_ref, mine_ref, taper_ref, cos_ref, sin_ref, second_ref, count_ref,
    own_ref, src_ref, turned, spec, shares, piece, rows_all, send_a, recv_a, send_b, recv_b,
):
    tables = (taper_ref, cos_ref, sin_ref, second_ref, count_ref)
    rows = traces_ref.shape[0]
    width = traces_ref.shape[1] // owners
    me, others = partners("chan", owners)
    greet([("chan", others[k]) for k in range(1, owners)])

    def cut(device):
        return pl.ds(pl.multiple_of(device * width, 128), width)

    def first(k):
        return remote(
            mine_ref.at[:, cut(others[k])], shares.at[k], send_a.at[k], recv_a.at[k], "chan", others[k]
        )

    def second(k):
        return remote(piece, rows_all.at[:, cut(me)], send_b.at[k], recv_b.at[k], "chan", others[k])

    for k in range(1, owners):
        first(k).start()

    @pl.loop(0, windows)
    def _(w):
        @pl.when(w == windows // 2)
        def _():
            total = mine_ref[:, cut(me)].astype(jnp.float32)
            for k in range(1, owners):
                first(k).wait()
                total = total + shares[k].astype(jnp.float32)
            piece[...] = total.astype(jnp.bfloat16)
            rows_all[:, cut(me)] = total.astype(jnp.bfloat16)
            for k in range(1, owners):
                second(k).start()

        def load(step, col):
            at = pl.ds(pl.multiple_of(step * 16, 16), 16)
            return traces_ref[at, pl.ds(pl.multiple_of(w * L + col, 128), 128)]

        def store(step, col, value):
            at = pl.ds(pl.multiple_of(w * rows + step * 16, 16), 16)
            own_ref[at, pl.ds(col, KA)] = value

        whiten_rows(load, store, tables, turned, spec)

    for k in range(1, owners):
        second(k).wait()

    def load(step, col):
        return rows_all[:, pl.ds(pl.multiple_of(step * L + col, 128), 128)]

    def store(step, col, value):
        src_ref[pl.ds(pl.multiple_of(step * 16, 16), 16), pl.ds(col, KA)] = value

    few = windows * rows_all.shape[0]
    whiten_rows(load, store, tables, turned.at[0 : 9 * few, :], spec.at[0 : 9 * few, :])


def whiten(traces, mine, owners, windows, tables):
    rows, sources = traces.shape[0], mine.shape[0]
    taper, tcos, tsin, second, rcount, _ = tables
    whole = pl.BlockSpec(memory_space=pltpu.VMEM)
    most = max(rows, windows * sources)
    width = windows * L // owners
    bf16 = jnp.bfloat16
    return pl.pallas_call(
        functools.partial(whiten_kernel, owners, windows),
        in_specs=[whole] * 7,
        out_specs=[whole] * 2,
        out_shape=[
            jax.ShapeDtypeStruct((windows * rows, L), bf16),
            jax.ShapeDtypeStruct((windows * sources, L), bf16),
        ],
        scratch_shapes=[
            pltpu.VMEM((9 * most, 2 * TA), bf16),
            pltpu.VMEM((9 * most, 4 * KA), jnp.float32),
            pltpu.VMEM((owners, sources, width), bf16),
            pltpu.VMEM((sources, width), bf16),
            pltpu.VMEM((sources, windows * L), bf16),
        ]
        + [pltpu.SemaphoreType.DMA((owners,))] * 4,
        compiler_params=pltpu.CompilerParams(collective_id=0, has_side_effects=True),
        name="whiten",
    )(traces, mine, taper, tcos, tsin, second, rcount)


def deliver_kernel(
    owners, shards, block, part_ref, send_ref, take_ref, out_ref,
    parts, totals, leaving, arrived, placed, final, send_a, recv_a, send_b, recv_b, send_c, recv_c,
):
    chan, chans = partners("chan", owners)
    time, times = partners("tm", shards)
    per = part_ref.shape[1] // block
    share = out_ref.shape[0]
    wide = per * LAGS
    greet([("tm", times[k]) for k in range(1, shards)] + [("chan", chans[k]) for k in range(1, owners)])

    def by_source(k):
        return remote(part_ref.at[times[k]], parts.at[k], send_a.at[k], recv_a.at[k], "tm", times[k])

    def by_owner(k):
        return remote(leaving.at[chans[k]], arrived.at[chan], send_b.at[k], recv_b.at[k], "chan", chans[k])

    def by_row(k):
        rows = pl.ds(pl.multiple_of(times[k] * share, share), share)
        return remote(placed.at[rows, :], final.at[time], send_c.at[k], recv_c.at[k], "tm", times[k])

    for k in range(1, shards):
        by_source(k).start()
    for k in range(1, shards):
        by_source(k).wait()
    for n in range(per):
        rows = pl.ds(n * block, block)
        total = part_ref[time, rows, :].astype(jnp.float32)
        for k in range(1, shards):
            total = total + parts[k, rows, :].astype(jnp.float32)
        totals[:, pl.ds(n * LAGS, LAGS)] = total.astype(jnp.bfloat16)

    for o in range(owners):
        value = jnp.dot(send_ref[o], totals[...], preferred_element_type=jnp.float32)
        leaving[o] = value.astype(jnp.bfloat16)
    for k in range(1, owners):
        by_owner(k).start()
    arrived[chan] = leaving[chan]
    for k in range(1, owners):
        by_owner(k).wait()

    if arrived.shape[1] % 16 == 0:
        got = jnp.dot(
            take_ref[...],
            arrived[...].reshape(owners * arrived.shape[1], wide),
            preferred_element_type=jnp.float32,
        )
    else:
        slots = arrived.shape[1]
        stacked = jnp.concatenate([arrived[o].astype(jnp.float32) for o in range(owners)], axis=0)
        got = jnp.dot(
            take_ref[...], stacked.astype(jnp.bfloat16), preferred_element_type=jnp.float32
        )
    placed[...] = got.astype(jnp.bfloat16)
    for k in range(1, shards):
        by_row(k).start()
    final[time] = placed[pl.ds(pl.multiple_of(time * share, share), share), :]
    for k in range(1, shards):
        by_row(k).wait()
    for m in range(shards):
        out_ref[:, pl.ds(m * wide, wide)] = final[m].astype(jnp.float32)


def deliver(partial, send, take, share):
    shards, rows, lags = partial.shape
    owners, slots, block = send.shape
    wide = rows // block * lags
    capacity = take.shape[0]
    whole = pl.BlockSpec(memory_space=pltpu.VMEM)
    bf16 = jnp.bfloat16
    return pl.pallas_call(
        functools.partial(deliver_kernel, owners, shards, block),
        in_specs=[whole] * 3,
        out_specs=whole,
        out_shape=jax.ShapeDtypeStruct((share, shards * wide), jnp.float32),
        scratch_shapes=[
            pltpu.VMEM((shards, rows, lags), bf16),
            pltpu.VMEM((block, wide), bf16),
            pltpu.VMEM((owners, slots, wide), bf16),
            pltpu.VMEM((owners, slots, wide), bf16),
            pltpu.VMEM((capacity, wide), bf16),
            pltpu.VMEM((shards, share, wide), bf16),
        ]
        + [pltpu.SemaphoreType.DMA((shards,))] * 2
        + [pltpu.SemaphoreType.DMA((owners,))] * 2
        + [pltpu.SemaphoreType.DMA((shards,))] * 2,
        compiler_params=pltpu.CompilerParams(collective_id=1, has_side_effects=True),
        name="deliver",
    )(partial, send, take)


def correlate_kernel(windows, sources, scale, own_ref, src_ref, inv_ref, o_ref, cross):
    chans = own_ref.shape[0] // windows

    @pl.loop(0, TB)
    def _(q):
        col_re = pl.ds(pl.multiple_of(q * 2 * KA, KA), KA)
        col_im = pl.ds(pl.multiple_of(q * 2 * KA + KA, KA), KA)
        for n in range(sources):
            s_re = [
                jnp.broadcast_to(src_ref[pl.ds(w * sources + n, 1), col_re], (16, KA)).astype(jnp.float32)
                for w in range(windows)
            ]
            s_im = [
                jnp.broadcast_to(src_ref[pl.ds(w * sources + n, 1), col_im], (16, KA)).astype(jnp.float32)
                for w in range(windows)
            ]
            for g in range(chans // 16):
                re = im = None
                for w in range(windows):
                    at = pl.ds(w * chans + g * 16, 16)
                    a = own_ref[at, col_re].astype(jnp.float32)
                    b = own_ref[at, col_im].astype(jnp.float32)
                    r = a * s_re[w] + b * s_im[w]
                    i = b * s_re[w] - a * s_im[w]
                    re = r if re is None else re + r
                    im = i if im is None else im + i
                at = pl.ds(n * chans + g * 16, 16)
                cross[at, col_re] = re.astype(jnp.bfloat16)
                cross[at, col_im] = im.astype(jnp.bfloat16)

    tile = math.gcd(sources * chans, 256)

    @pl.loop(0, sources * chans // tile)
    def _(step):
        at = pl.ds(pl.multiple_of(step * tile, tile), tile)
        out = jnp.dot(cross[at, :], inv_ref[...], preferred_element_type=jnp.float32)
        o_ref[at, :] = (out * scale).astype(jnp.bfloat16)


def correlate(own, src, windows, scale, tables):
    chans, sources = own.shape[0] // windows, src.shape[0] // windows
    inverse = tables[5]
    whole = pl.BlockSpec(memory_space=pltpu.VMEM)
    return pl.pallas_call(
        functools.partial(correlate_kernel, windows, sources, scale),
        in_specs=[whole] * 3,
        out_specs=whole,
        out_shape=jax.ShapeDtypeStruct((sources * chans, LAGS), jnp.bfloat16),
        scratch_shapes=[pltpu.VMEM((sources * chans, L), jnp.bfloat16)],
        name="correlate",
    )(own, src, inverse)


def body(raw_traces, owner_lists, source_owner, source_slot):
    block, windows, length = raw_traces.shape
    owners = lax.axis_size("chan")
    shards = lax.axis_size("tm")
    capacity = owner_lists.shape[1]
    slots = (capacity + owners - 1) // owners
    share = capacity // shards
    me = lax.axis_index("chan")
    tables = tuple(jnp.asarray(t) for t in make_tables())
    scale = 1.0 / math.sqrt(windows * shards * HALF)
    bf16, f32 = jnp.bfloat16, jnp.float32

    traces = raw_traces.reshape(block, windows * length)
    ids = owner_lists[source_owner[:, None], source_slot].reshape(-1)
    sources = ids.shape[0]
    pick = (ids[:, None] == me * block + jnp.arange(block)[None, :]).astype(bf16)
    mine = jnp.dot(pick, traces, preferred_element_type=f32).astype(bf16)
    own, src = whiten(traces, mine, owners, windows, tables)
    partial = correlate(own, src, windows, scale, tables)
    per = sources // shards

    source_block = jnp.floor_divide(owner_lists, block)
    matched = (owner_lists >= 0) & (source_block == me)
    rank = jnp.cumsum(matched.astype(jnp.int32), axis=1) - 1
    slot_ids = jnp.arange(slots, dtype=jnp.int32)
    chosen = matched[:, None, :] & (rank[:, None, :] == slot_ids[None, :, None])
    wanted = jnp.sum(jnp.where(chosen, owner_lists[:, None, :] - me * block + 1, 0), axis=2) - 1
    send = (wanted[:, :, None] == jnp.arange(block)[None, None, :]).astype(bf16)

    my_list = lax.dynamic_index_in_dim(owner_lists, me, 0, keepdims=False)
    my_block = jnp.floor_divide(my_list, block)
    live = my_list >= 0
    position = jnp.arange(capacity, dtype=jnp.int32)
    same = (my_block[:, None] == my_block[None, :]) & (position[None, :] < position[:, None]) & live[None, :]
    earlier = jnp.sum(same.astype(jnp.int32), axis=1)
    take = (
        live[:, None, None]
        & (my_block[:, None, None] == jnp.arange(owners)[None, :, None])
        & (earlier[:, None, None] == slot_ids[None, None, :])
    ).astype(bf16)
    result = deliver(
        partial.reshape(shards, per * block, LAGS), send, take.reshape(capacity, owners * slots), share
    )
    return result.reshape(share, sources, LAGS)


def solution(mesh):
    return jax.shard_map(
        body,
        mesh=mesh,
        in_specs=(P("chan", "tm", None), P(), P(), P()),
        out_specs=P(("chan", "tm"), None, None),
        check_vma=False,
    )
```

```python
import functools
import math

import jax
import jax.numpy as jnp
import numpy as np
from jax import lax
from jax.experimental import pallas as pl
from jax.experimental.pallas import tpu as pltpu
from jax.sharding import PartitionSpec as P

L = 4096
HALF = L // 2
HW = 64
LAGS = 256
EPSILON = 1e-06
TB = 16
TA = L // TB
KA = HALF // TB


def make_tables():
    a = np.arange(TA, dtype=np.int64)
    taper = 0.5 - 0.5 * np.cos(2 * np.pi / L * (np.arange(L) + 0.5))
    kb = np.arange(TB // 2 + 1, dtype=np.int64)
    twist = 2 * np.pi / L * (kb[:, None] * a[None, :])
    twist_cos, twist_sin = np.cos(twist), np.sin(twist)
    ka = np.arange(KA, dtype=np.int64)
    low = 2 * np.pi / TA * (a[:, None] * ka[None, :] % TA)
    high = 2 * np.pi / TA * (a[:, None] * (TA - 1 - ka)[None, :] % TA)
    top = [np.cos(low), -np.sin(low), np.cos(high), np.sin(high)]
    bottom = [np.sin(low), np.cos(low), np.sin(high), -np.cos(high)]
    second = np.concatenate([np.concatenate(top, 1), np.concatenate(bottom, 1)], 0)
    bins = np.arange(TB)[:, None] + TB * ka[None, :]
    counts = np.minimum(bins, HW) + np.minimum(HALF - 1 - bins, HW) + 1
    lag = np.arange(LAGS, dtype=np.int64) - LAGS // 2
    angle = 2 * np.pi / L * (bins[:, :, None] * lag % L)
    weight = np.where(bins == 0, 1.0, 2.0)[:, :, None]
    inverse = np.stack([weight * np.cos(angle), -weight * np.sin(angle)], 1)
    f32 = np.float32
    return (
        taper.astype(f32)[None, :],
        twist_cos.astype(f32),
        twist_sin.astype(f32),
        second.astype(jnp.bfloat16),
        (1.0 / counts).astype(f32),
        inverse.reshape(L, LAGS).astype(jnp.bfloat16),
    )


def dft4(x0, x1, x2, x3):
    if x0[1] is None:
        s, d = x0[0] + x2[0], x0[0] - x2[0]
        u, v = x1[0] + x3[0], x1[0] - x3[0]
        return (s + u, None), (d, -v), (s - u, None), (d, v)
    sr, si, dr, di = x0[0] + x2[0], x0[1] + x2[1], x0[0] - x2[0], x0[1] - x2[1]
    ur, ui, vr, vi = x1[0] + x3[0], x1[1] + x3[1], x1[0] - x3[0], x1[1] - x3[1]
    return (sr + ur, si + ui), (dr + vi, di - vr), (sr - ur, si - ui), (dr - vi, di + vr)


def turn(value, step):
    c, s = math.cos(2 * math.pi * step / TB), math.sin(2 * math.pi * step / TB)
    re, im = value
    if step == 0:
        return value
    if im is None:
        return re * c, re * (-s)
    return re * c + im * s, im * c - re * s


def dft16_real(x):
    first = [dft4(*[(x[n + 4 * m], None) for m in range(4)]) for n in range(4)]
    out = [None] * 9
    for q in range(3):
        parts = [turn(first[n][q], n * q) for n in range(4)]
        if q == 0:
            r = [p[0] for p in parts]
            out[0] = (r[0] + r[1] + r[2] + r[3], None)
            out[4] = (r[0] - r[2], r[3] - r[1])
            out[8] = ((r[0] + r[2]) - (r[1] + r[3]), None)
        else:
            if parts[0][1] is None:
                parts[0] = (parts[0][0], jnp.zeros_like(parts[0][0]))
            y = dft4(*parts)
            out[q] = y[0]
            out[q + 4] = y[1]
            if q == 1:
                out[3] = (y[3][0], -y[3][1])
            else:
                pass
    parts = [turn(first[n][1], n) for n in range(4)]
    y = dft4(*parts)
    out[7] = (y[2][0], -y[2][1])
    return out


def whiten_rows(load, store, tables, turned, spec):
    taper_ref, cos_ref, sin_ref, second_ref, count_ref = tables
    rows = turned.shape[0] // 9
    place = {q: (q - 1) * rows for q in range(1, 9)}
    place[0] = 8 * rows
    group = 16

    @pl.loop(0, rows // group)
    def _(step):
        base = pl.multiple_of(step * group, group)
        for h in range(TA // 128):
            x = []
            for b in range(TB):
                cols = pl.ds(b * TA + h * 128, 128)
                v = load(step, b * TA + h * 128).astype(jnp.float32) * taper_ref[:, cols]
                x.append(v.astype(jnp.bfloat16).astype(jnp.float32))
            y = dft16_real(x)
            here = pl.ds(h * 128, 128)
            there = pl.ds(TA + h * 128, 128)
            for q in range(TB // 2 + 1):
                re, im = y[q]
                target = pl.ds(pl.multiple_of(base + place[q], group), group)
                if q == 0:
                    out_re, out_im = re, jnp.zeros_like(re)
                else:
                    c, s = cos_ref[pl.ds(q, 1), here], sin_ref[pl.ds(q, 1), here]
                    if im is None:
                        out_re, out_im = re * c, -(re * s)
                    else:
                        out_re, out_im = re * c + im * s, im * c - re * s
                turned[target, here] = out_re.astype(jnp.bfloat16)
                turned[target, there] = out_im.astype(jnp.bfloat16)

    split = 7 * rows
    spec[0:split, :] = jnp.dot(
        turned[0:split, :], second_ref[...], preferred_element_type=jnp.float32
    )
    spec[split:, 0 : 2 * KA] = jnp.dot(
        turned[split:, :], second_ref[:, 0 : 2 * KA], preferred_element_type=jnp.float32
    )

    lane = lax.broadcasted_iota(jnp.int32, (8, KA), 1)

    def ahead(v, d):
        return jnp.where(lane < KA - d, pltpu.roll(v, KA - d, 1), 0.0)

    def behind(v, d):
        return jnp.where(lane >= d, pltpu.roll(v, d, 1), 0.0)

    @pl.loop(0, rows // 16)
    def _(step):
        done = [[], []]
        for half in range(2):
            base = pl.multiple_of(step * 16, 16) + half * 8

            def part(q, imag):
                src, col = (q, 0) if q <= 8 else (TB - q, 2 * KA)
                at = pl.ds(pl.multiple_of(base + place[src], 8), 8)
                return spec[at, pl.ds(col + imag * KA, KA)]

            mags = []
            for q in range(TB):
                re, im = part(q, 0), part(q, 1)
                m = jnp.sqrt(re * re + im * im)
                mags.append(m.astype(jnp.bfloat16).astype(jnp.float32))
            prefix = [mags[0]]
            for q in range(1, TB):
                prefix.append(prefix[-1] + mags[q])
            total = prefix[-1]
            near = total
            for d in (1, 2, 3):
                near = near + ahead(total, d) + behind(total, d)
            suffix = total
            for q in range(TB):
                smooth = near + behind(suffix, 4) + ahead(prefix[q], 4)
                suffix = suffix - mags[q]
                inv = 1.0 / (smooth * count_ref[pl.ds(q, 1), :] + EPSILON)
                done[half].append((part(q, 0) * inv, part(q, 1) * inv))
        for q in range(TB):
            for p in range(2):
                both = jnp.concatenate([done[0][q][p], done[1][q][p]], axis=0)
                store(step, q * 2 * KA + p * KA, both.astype(jnp.bfloat16))


def partners(axis, extent):
    me = lax.axis_index(axis)
    return me, [lax.rem(me + k, extent) for k in range(extent)]


def remote(src, dst, send, recv, axis, device):
    return pltpu.make_async_remote_copy(
        src_ref=src,
        dst_ref=dst,
        send_sem=send,
        recv_sem=recv,
        device_id={axis: device},
        device_id_type=pl.DeviceIdType.MESH,
    )


def greet(pairs):
    barrier = pltpu.get_barrier_semaphore()
    for axis, device in pairs:
        pl.semaphore_signal(
            barrier, inc=1, device_id={axis: device}, device_id_type=pl.DeviceIdType.MESH
        )
    pl.semaphore_wait(barrier, len(pairs))


PIECES = 2


def kernel(
    owners, shards, block, windows, scale,
    traces_ref, mine_ref, send_ref, take_ref, taper_ref, cos_ref, sin_ref, second_ref, count_ref, inv_hbm,
    out_ref,
    turned, spec, own, source, cross, inv_ref, shares, piece, gathered, part, parts, totals,
    leaving, arrived, placed, final,
    inv_sem, send_r, recv_r, send_g, recv_g, send_a, recv_a, send_b, recv_b, send_c, recv_c,
):
    tables = (taper_ref, cos_ref, sin_ref, second_ref, count_ref)
    f32, bf16 = jnp.float32, jnp.bfloat16
    chunks, group, _ = mine_ref.shape
    held = group // windows
    width = L // owners
    per = part.shape[1] // block
    ends = held // per
    share = out_ref.shape[0]
    wide = totals.shape[2]
    chan, chans = partners("chan", owners)
    time, times = partners("tm", shards)
    home = time // ends
    greet([("chan", chans[k]) for k in range(1, owners)] + [("tm", times[k]) for k in range(1, shards)])

    def cut(device):
        return pl.ds(pl.multiple_of(device * width, 128), width)

    def chunk_of(s):
        return lax.rem(home + 1 + s, chunks)

    def reduce_copy(s, k):
        src = mine_ref.at[chunk_of(s), :, cut(chans[k])]
        return remote(src, shares.at[s, k], send_r.at[s, k], recv_r.at[s, k], "chan", chans[k])

    def gather_copy(s, k):
        dst = gathered.at[s, :, cut(chan)]
        return remote(piece.at[s], dst, send_g.at[s, k], recv_g.at[s, k], "chan", chans[k])

    for s in range(chunks):
        for k in range(1, owners):
            reduce_copy(s, k).start()
    inv_copy = pltpu.make_async_copy(inv_hbm, inv_ref, inv_sem)
    inv_copy.start()

    @pl.loop(0, windows)
    def _(w):
        def load(step, col):
            at = pl.ds(pl.multiple_of(w * block + step * group, group), group)
            return traces_ref[at, pl.ds(col, 128)]

        def store(step, col, value):
            at = pl.ds(pl.multiple_of(w * block + step * group, group), group)
            own[at, pl.ds(col, KA)] = value.astype(f32)

        whiten_rows(load, store, tables, turned, spec)

        total = mine_ref[chunk_of(w), :, cut(chan)].astype(f32)
        for k in range(1, owners):
            reduce_copy(w, k).wait()
            total = total + shares[w, k].astype(f32)
        piece[w] = total.astype(bf16)
        gathered[w, :, cut(chan)] = total.astype(bf16)
        for k in range(1, owners):
            gather_copy(w, k).start()

    inv_copy.wait()

    @pl.loop(0, chunks)
    def _(s):
        for k in range(1, owners):
            gather_copy(s, k).wait()

        def load(step, col):
            return gathered[s, :, pl.ds(col, 128)]

        def store(step, col, value):
            source[:, pl.ds(col, KA)] = value.astype(f32)

        whiten_rows(load, store, tables, turned.at[0 : 9 * group, :], spec.at[0 : 9 * group, :])

        @pl.loop(0, TB)
        def _(q):
            col_re = pl.ds(pl.multiple_of(q * 2 * KA, KA), KA)
            col_im = pl.ds(pl.multiple_of(q * 2 * KA + KA, KA), KA)
            rows = [[pl.ds(w * held + n, 1) for w in range(windows)] for n in range(held)]
            wave = [[(source[r, col_re], source[r, col_im]) for r in line] for line in rows]
            wave = [
                [tuple(jnp.broadcast_to(v, (16, KA)) for v in (x, y, x - y)) for x, y in line]
                for line in wave
            ]
            for g in range(block // 16):
                at = [pl.ds(w * block + g * 16, 16) for w in range(windows)]
                a = [own[r, col_re] for r in at]
                b = [own[r, col_im] for r in at]
                c = [x + y for x, y in zip(a, b)]
                for n in range(held):
                    sums = []
                    for factor, which in ((a, 0), (b, 1), (c, 2)):
                        total = factor[0] * wave[n][0][which]
                        for w in range(1, windows):
                            total = total + factor[w] * wave[n][w][which]
                        sums.append(total)
                    to = pl.ds(n * block + g * 16, 16)
                    cross[to, col_re] = (sums[0] + sums[1]).astype(bf16)
                    cross[to, col_im] = (sums[2] - sums[0] + sums[1]).astype(bf16)

        out = jnp.dot(cross[...], inv_ref[...], preferred_element_type=f32) * scale
        out = out.astype(bf16)
        for j in range(ends):
            end = chunk_of(s) * ends + j
            part[end] = out[j * per * block : (j + 1) * per * block]
            k = lax.rem(end - time + shards, shards)

            @pl.when(k != 0)
            def _():
                remote(part.at[end], parts.at[k], send_a.at[k], recv_a.at[k], "tm", end).start()

    def by_source(k):
        return remote(part.at[times[k]], parts.at[k], send_a.at[k], recv_a.at[k], "tm", times[k])

    def by_owner(p, k):
        src, dst = leaving.at[p, chans[k]], arrived.at[p, chan]
        return remote(src, dst, send_b.at[p, k], recv_b.at[p, k], "chan", chans[k])

    def by_row(p, k):
        rows = pl.ds(pl.multiple_of(times[k] * share, share), share)
        src, dst = placed.at[p, rows, :], final.at[p, time]
        return remote(src, dst, send_c.at[p, k], recv_c.at[p, k], "tm", times[k])

    for k in range(1, shards):
        by_source(k).wait()
    each = per // PIECES
    for p in range(PIECES):
        for n in range(each):
            rows = pl.ds((p * each + n) * block, block)
            total = part[time, rows, :].astype(f32)
            for k in range(1, shards):
                total = total + parts[k, rows, :].astype(f32)
            totals[p, :, pl.ds(n * LAGS, LAGS)] = total.astype(bf16)
        for o in range(owners):
            leaving[p, o] = jnp.dot(send_ref[o], totals[p], preferred_element_type=f32).astype(bf16)
        for k in range(1, owners):
            by_owner(p, k).start()
        arrived[p, chan] = leaving[p, chan]

    slots = arrived.shape[2]
    for p in range(PIECES):
        for k in range(1, owners):
            by_owner(p, k).wait()
        if slots % 16 == 0:
            stacked = arrived[p].reshape(owners * slots, wide)
        else:
            stacked = jnp.concatenate([arrived[p, o].astype(f32) for o in range(owners)], axis=0).astype(bf16)
        placed[p] = jnp.dot(take_ref[...], stacked, preferred_element_type=f32).astype(bf16)
        for k in range(1, shards):
            by_row(p, k).start()
        final[p, time] = placed[p, pl.ds(pl.multiple_of(time * share, share), share), :]
    for p in range(PIECES):
        for k in range(1, shards):
            by_row(p, k).wait()
        for m in range(shards):
            out_ref[:, pl.ds((m * PIECES + p) * wide, wide)] = final[p, m].astype(f32)


def run(traces, mine, send, take, shards, share, scale, tables):
    chunks, group, _ = mine.shape
    owners, slots, block = send.shape
    windows = traces.shape[0] // block
    held = group // windows
    sources = chunks * held
    per = sources // shards
    wide = per // PIECES * LAGS
    capacity = take.shape[0]
    most = max(block, group)
    vmem = pl.BlockSpec(memory_space=pltpu.VMEM)
    bf16, f32 = jnp.bfloat16, jnp.float32
    sems = lambda *shape: [pltpu.SemaphoreType.DMA(shape)] * 2
    return pl.pallas_call(
        functools.partial(kernel, owners, shards, block, windows, scale),
        in_specs=[vmem] * 9 + [pl.BlockSpec(memory_space=pl.ANY)],
        out_specs=vmem,
        out_shape=jax.ShapeDtypeStruct((share, sources * LAGS), f32),
        scratch_shapes=[
            pltpu.VMEM((9 * most, 2 * TA), bf16),
            pltpu.VMEM((9 * most, 4 * KA), f32),
            pltpu.VMEM((windows * block, L), f32),
            pltpu.VMEM((group, L), f32),
            pltpu.VMEM((held * block, L), bf16),
            pltpu.VMEM((L, LAGS), bf16),
            pltpu.VMEM((chunks, owners, group, L // owners), bf16),
            pltpu.VMEM((chunks, group, L // owners), bf16),
            pltpu.VMEM((chunks, group, L), bf16),
            pltpu.VMEM((shards, per * block, LAGS), bf16),
            pltpu.VMEM((shards, per * block, LAGS), bf16),
            pltpu.VMEM((PIECES, block, wide), bf16),
            pltpu.VMEM((PIECES, owners, slots, wide), bf16),
            pltpu.VMEM((PIECES, owners, slots, wide), bf16),
            pltpu.VMEM((PIECES, capacity, wide), bf16),
            pltpu.VMEM((PIECES, shards, share, wide), bf16),
            pltpu.SemaphoreType.DMA,
        ]
        + sems(chunks, owners) + sems(chunks, owners)
        + sems(shards) + sems(PIECES, owners) + sems(PIECES, shards),
        compiler_params=pltpu.CompilerParams(collective_id=0, has_side_effects=True),
        name="correlations",
    )(traces, mine, send, take, *tables)


def body(raw_traces, owner_lists, source_owner, source_slot):
    block, windows, length = raw_traces.shape
    owners = lax.axis_size("chan")
    shards = lax.axis_size("tm")
    capacity = owner_lists.shape[1]
    slots = (capacity + owners - 1) // owners
    share = capacity // shards
    me = lax.axis_index("chan")
    tables = tuple(jnp.asarray(t) for t in make_tables())
    scale = 1.0 / math.sqrt(windows * shards * HALF)
    bf16, f32 = jnp.bfloat16, jnp.float32

    held = 16 // windows
    ids = owner_lists[source_owner[:, None], source_slot].reshape(-1)
    sources = ids.shape[0]
    chunks = sources // held
    assert chunks == windows and held % (sources // shards) == 0
    traces = jnp.transpose(raw_traces, (1, 0, 2)).reshape(windows * block, length)
    channel = jnp.broadcast_to(ids.reshape(chunks, 1, held) - me * block, (chunks, windows, held))
    inside = (channel >= 0) & (channel < block)
    row = jnp.where(inside, channel + block * jnp.arange(windows, dtype=jnp.int32)[None, :, None], -1)
    pick = (row.reshape(-1)[:, None] == jnp.arange(windows * block, dtype=jnp.int32)[None, :]).astype(bf16)
    mine = jnp.dot(pick, traces, preferred_element_type=f32).astype(bf16)
    mine = mine.reshape(chunks, windows * held, length)

    source_block = jnp.floor_divide(owner_lists, block)
    matched = (owner_lists >= 0) & (source_block == me)
    rank = jnp.cumsum(matched.astype(jnp.int32), axis=1) - 1
    slot_ids = jnp.arange(slots, dtype=jnp.int32)
    chosen = matched[:, None, :] & (rank[:, None, :] == slot_ids[None, :, None])
    wanted = jnp.sum(jnp.where(chosen, owner_lists[:, None, :] - me * block + 1, 0), axis=2) - 1
    send = (wanted[:, :, None] == jnp.arange(block)[None, None, :]).astype(bf16)

    my_list = lax.dynamic_index_in_dim(owner_lists, me, 0, keepdims=False)
    my_block = jnp.floor_divide(my_list, block)
    live = my_list >= 0
    position = jnp.arange(capacity, dtype=jnp.int32)
    same = (my_block[:, None] == my_block[None, :]) & (position[None, :] < position[:, None]) & live[None, :]
    earlier = jnp.sum(same.astype(jnp.int32), axis=1)
    take = (
        live[:, None, None]
        & (my_block[:, None, None] == jnp.arange(owners)[None, :, None])
        & (earlier[:, None, None] == slot_ids[None, None, :])
    ).astype(bf16)
    result = run(
        traces, mine, send, take.reshape(capacity, owners * slots), shards, share, scale, tables
    )
    return result.reshape(share, sources, LAGS)


def solution(mesh):
    return jax.shard_map(
        body,
        mesh=mesh,
        in_specs=(P("chan", "tm", None), P(), P(), P()),
        out_specs=P(("chan", "tm"), None, None),
        check_vma=False,
    )
```

```python
import functools
import math

import jax
import jax.numpy as jnp
import numpy as np
from jax import lax
from jax.experimental import pallas as pl
from jax.experimental.pallas import tpu as pltpu
from jax.sharding import PartitionSpec as P

L = 4096
HALF = L // 2
HW = 64
LAGS = 256
EPSILON = 1e-06
TB = 16
TA = L // TB
KA = HALF // TB


def make_tables():
    a = np.arange(TA, dtype=np.int64)
    taper = 0.5 - 0.5 * np.cos(2 * np.pi / L * (np.arange(L) + 0.5))
    kb = np.arange(TB // 2 + 1, dtype=np.int64)
    twist = 2 * np.pi / L * (kb[:, None] * a[None, :])
    twist_cos, twist_sin = np.cos(twist), np.sin(twist)
    ka = np.arange(KA, dtype=np.int64)
    low = 2 * np.pi / TA * (a[:, None] * ka[None, :] % TA)
    high = 2 * np.pi / TA * (a[:, None] * (TA - 1 - ka)[None, :] % TA)
    top = [np.cos(low), -np.sin(low), np.cos(high), np.sin(high)]
    bottom = [np.sin(low), np.cos(low), np.sin(high), -np.cos(high)]
    second = np.concatenate([np.concatenate(top, 1), np.concatenate(bottom, 1)], 0)
    bins = np.arange(TB)[:, None] + TB * ka[None, :]
    counts = np.minimum(bins, HW) + np.minimum(HALF - 1 - bins, HW) + 1
    lag = np.arange(LAGS, dtype=np.int64) - LAGS // 2
    angle = 2 * np.pi / L * (bins[:, :, None] * lag % L)
    weight = np.where(bins == 0, 1.0, 2.0)[:, :, None]
    inverse = np.stack([weight * np.cos(angle), -weight * np.sin(angle)], 1)
    f32 = np.float32
    return (
        taper.astype(f32)[None, :],
        twist_cos.astype(f32),
        twist_sin.astype(f32),
        second.astype(jnp.bfloat16),
        (1.0 / counts).astype(f32),
        inverse.reshape(L, LAGS).astype(jnp.bfloat16),
    )


def dft4(x0, x1, x2, x3):
    if x0[1] is None:
        s, d = x0[0] + x2[0], x0[0] - x2[0]
        u, v = x1[0] + x3[0], x1[0] - x3[0]
        return (s + u, None), (d, -v), (s - u, None), (d, v)
    sr, si, dr, di = x0[0] + x2[0], x0[1] + x2[1], x0[0] - x2[0], x0[1] - x2[1]
    ur, ui, vr, vi = x1[0] + x3[0], x1[1] + x3[1], x1[0] - x3[0], x1[1] - x3[1]
    return (sr + ur, si + ui), (dr + vi, di - vr), (sr - ur, si - ui), (dr - vi, di + vr)


def turn(value, step):
    c, s = math.cos(2 * math.pi * step / TB), math.sin(2 * math.pi * step / TB)
    re, im = value
    if step == 0:
        return value
    if im is None:
        return re * c, re * (-s)
    return re * c + im * s, im * c - re * s


def dft16_real(x):
    first = [dft4(*[(x[n + 4 * m], None) for m in range(4)]) for n in range(4)]
    out = [None] * 9
    for q in range(3):
        parts = [turn(first[n][q], n * q) for n in range(4)]
        if q == 0:
            r = [p[0] for p in parts]
            out[0] = (r[0] + r[1] + r[2] + r[3], None)
            out[4] = (r[0] - r[2], r[3] - r[1])
            out[8] = ((r[0] + r[2]) - (r[1] + r[3]), None)
        else:
            if parts[0][1] is None:
                parts[0] = (parts[0][0], jnp.zeros_like(parts[0][0]))
            y = dft4(*parts)
            out[q] = y[0]
            out[q + 4] = y[1]
            if q == 1:
                out[3] = (y[3][0], -y[3][1])
            else:
                pass
    parts = [turn(first[n][1], n) for n in range(4)]
    y = dft4(*parts)
    out[7] = (y[2][0], -y[2][1])
    return out


def whiten_rows(load, store, tables, turned, spec):
    taper_ref, cos_ref, sin_ref, second_ref, count_ref = tables
    rows = turned.shape[0] // 9
    place = {q: (q - 1) * rows for q in range(1, 9)}
    place[0] = 8 * rows
    group = 16

    @pl.loop(0, rows // group)
    def _(step):
        base = pl.multiple_of(step * group, group)
        for h in range(TA // 128):
            x = []
            for b in range(TB):
                cols = pl.ds(b * TA + h * 128, 128)
                v = load(step, b * TA + h * 128).astype(jnp.float32) * taper_ref[:, cols]
                x.append(v.astype(jnp.bfloat16).astype(jnp.float32))
            y = dft16_real(x)
            here = pl.ds(h * 128, 128)
            there = pl.ds(TA + h * 128, 128)
            for q in range(TB // 2 + 1):
                re, im = y[q]
                target = pl.ds(pl.multiple_of(base + place[q], group), group)
                if q == 0:
                    out_re, out_im = re, jnp.zeros_like(re)
                else:
                    c, s = cos_ref[pl.ds(q, 1), here], sin_ref[pl.ds(q, 1), here]
                    if im is None:
                        out_re, out_im = re * c, -(re * s)
                    else:
                        out_re, out_im = re * c + im * s, im * c - re * s
                turned[target, here] = out_re.astype(jnp.bfloat16)
                turned[target, there] = out_im.astype(jnp.bfloat16)

    split = 7 * rows
    spec[0:split, :] = jnp.dot(
        turned[0:split, :], second_ref[...], preferred_element_type=jnp.float32
    )
    spec[split:, 0 : 2 * KA] = jnp.dot(
        turned[split:, :], second_ref[:, 0 : 2 * KA], preferred_element_type=jnp.float32
    )

    lane = lax.broadcasted_iota(jnp.int32, (8, KA), 1)

    def ahead(v, d):
        return jnp.where(lane < KA - d, pltpu.roll(v, KA - d, 1), 0.0)

    def behind(v, d):
        return jnp.where(lane >= d, pltpu.roll(v, d, 1), 0.0)

    @pl.loop(0, rows // 16)
    def _(step):
        done = [[], []]
        for half in range(2):
            base = pl.multiple_of(step * 16, 16) + half * 8

            def part(q, imag):
                src, col = (q, 0) if q <= 8 else (TB - q, 2 * KA)
                at = pl.ds(pl.multiple_of(base + place[src], 8), 8)
                return spec[at, pl.ds(col + imag * KA, KA)]

            mags = []
            for q in range(TB):
                re, im = part(q, 0), part(q, 1)
                m = jnp.sqrt(re * re + im * im)
                mags.append(m.astype(jnp.bfloat16).astype(jnp.float32))
            prefix = [mags[0]]
            for q in range(1, TB):
                prefix.append(prefix[-1] + mags[q])
            total = prefix[-1]
            near = total
            for d in (1, 2, 3):
                near = near + ahead(total, d) + behind(total, d)
            suffix = total
            for q in range(TB):
                smooth = near + behind(suffix, 4) + ahead(prefix[q], 4)
                suffix = suffix - mags[q]
                inv = 1.0 / (smooth * count_ref[pl.ds(q, 1), :] + EPSILON)
                done[half].append((part(q, 0) * inv, part(q, 1) * inv))
        for q in range(TB):
            for p in range(2):
                both = jnp.concatenate([done[0][q][p], done[1][q][p]], axis=0)
                store(step, q * 2 * KA + p * KA, both.astype(jnp.bfloat16))


def partners(axis, extent):
    me = lax.axis_index(axis)
    return me, [lax.rem(me + k, extent) for k in range(extent)]


def remote(src, dst, send, recv, axis, device):
    return pltpu.make_async_remote_copy(
        src_ref=src,
        dst_ref=dst,
        send_sem=send,
        recv_sem=recv,
        device_id={axis: device},
        device_id_type=pl.DeviceIdType.MESH,
    )


def greet(pairs):
    barrier = pltpu.get_barrier_semaphore()
    for axis, device in pairs:
        pl.semaphore_signal(
            barrier, inc=1, device_id={axis: device}, device_id_type=pl.DeviceIdType.MESH
        )
    return lambda: pl.semaphore_wait(barrier, len(pairs))


PIECES = 2


def kernel(
    owners, shards, block, windows, scale,
    slots, traces_ref, lists_ref, lists_s, owner_s, slot_s, taper_ref, cos_ref, sin_ref, second_ref, count_ref, inv_hbm,
    out_ref,
    mine_ref, send_ref, take_ref, turned, spec, own, source, cross, inv_ref, shares, piece, gathered, part, parts, totals,
    leaving, arrived, placed, final,
    inv_sem, send_r, recv_r, send_g, recv_g, send_a, recv_a, send_b, recv_b, send_c, recv_c,
):
    tables = (taper_ref, cos_ref, sin_ref, second_ref, count_ref)
    f32, bf16 = jnp.float32, jnp.bfloat16
    chunks, group, _ = mine_ref.shape
    held = group // windows
    width = L // owners
    per = part.shape[1] // block
    ends = held // per
    share = out_ref.shape[0]
    wide = totals.shape[2]
    chan, chans = partners("chan", owners)
    time, times = partners("tm", shards)
    home = time // ends
    pairs = [("chan", chans[k]) for k in range(1, owners)] + [("tm", times[k]) for k in range(1, shards)]
    all_here = greet(pairs)

    def iota(shape, dim):
        return lax.broadcasted_iota(jnp.int32, shape, dim)

    shape = (chunks * group, windows * block)
    row, col = iota(shape, 0), iota(shape, 1)
    which = row // group * held + row % held
    wanted = jnp.full(shape, -1, jnp.int32)
    steps, each_step = slot_s.shape
    for i in range(steps * each_step):
        channel = lists_s[owner_s[i // each_step], slot_s[i // each_step, i % each_step]]
        wanted = jnp.where(which == i, channel, wanted)
    hit = (wanted == chan * block + col % block) & (col // block == row // held % windows)
    pick = jnp.where(hit, 1.0, 0.0).astype(bf16)

    @pl.loop(0, L // 1024)
    def _(t):
        at = pl.ds(pl.multiple_of(t * 1024, 1024), 1024)
        rows = jnp.dot(pick, traces_ref[:, at], preferred_element_type=f32).astype(bf16)
        for g in range(chunks):
            mine_ref[g, :, at] = rows[g * group : (g + 1) * group]

    all_here()

    def cut(device):
        return pl.ds(pl.multiple_of(device * width, 128), width)

    def chunk_of(s):
        return lax.rem(home + 1 + s, chunks)

    def reduce_copy(s, k):
        src = mine_ref.at[chunk_of(s), :, cut(chans[k])]
        return remote(src, shares.at[s, k], send_r.at[s, k], recv_r.at[s, k], "chan", chans[k])

    def gather_copy(s, k):
        dst = gathered.at[s, :, cut(chan)]
        return remote(piece.at[s], dst, send_g.at[s, k], recv_g.at[s, k], "chan", chans[k])

    for s in range(2):
        for k in range(1, owners):
            reduce_copy(s, k).start()
    inv_copy = pltpu.make_async_copy(inv_hbm, inv_ref, inv_sem)
    inv_copy.start()

    capacity = lists_ref.shape[1]
    before = jnp.where(iota((capacity, capacity), 0) <= iota((capacity, capacity), 1), 1.0, 0.0)
    lists = lists_ref[...]
    here = (lists >= chan * block) & (lists < (chan + 1) * block)
    inside = jnp.where(here, lists - chan * block, -1).astype(f32)
    wall = (owners * slots, capacity)
    spread = jnp.where(
        iota((owners * slots, owners), 0) // slots == iota((owners * slots, owners), 1), 1.0, 0.0
    )
    offset = jnp.dot(spread, inside, preferred_element_type=f32)
    live = offset >= 0
    slot = (iota(wall, 0) % slots + 1).astype(f32)
    rank = jnp.dot(jnp.where(live, 1.0, 0.0), before, preferred_element_type=f32)
    channel = jnp.sum(jnp.where(live & (rank == slot), offset + 1.0, 0.0), axis=1, keepdims=True) - 1.0
    send_ref[...] = jnp.where(
        channel == iota((owners * slots, block), 1).astype(f32), 1.0, 0.0
    )
    listed = jnp.broadcast_to(lists_ref[pl.ds(chan, 1), :], wall)
    start = iota(wall, 0) // slots * block
    found = (listed >= start) & (listed < start + block)
    rank = jnp.dot(jnp.where(found, 1.0, 0.0), before, preferred_element_type=f32)
    take = jnp.where(found & (rank == slot), 1.0, 0.0)
    take_ref[...] = take.T.astype(bf16)

    @pl.loop(0, windows)
    def _(w):
        def load(step, col):
            at = pl.ds(pl.multiple_of(w * block + step * group, group), group)
            return traces_ref[at, pl.ds(col, 128)]

        def store(step, col, value):
            at = pl.ds(pl.multiple_of(w * block + step * group, group), group)
            own[at, pl.ds(col, KA)] = value.astype(f32)

        whiten_rows(load, store, tables, turned, spec)

        total = mine_ref[chunk_of(w), :, cut(chan)].astype(f32)
        for k in range(1, owners):
            reduce_copy(w, k).wait()
            total = total + shares[w, k].astype(f32)
        piece[w] = total.astype(bf16)
        gathered[w, :, cut(chan)] = total.astype(bf16)
        for k in range(1, owners):
            gather_copy(w, k).start()

        @pl.when(w + 2 < chunks)
        def _():
            for k in range(1, owners):
                reduce_copy(w + 2, k).start()

    inv_copy.wait()

    @pl.loop(0, chunks)
    def _(s):
        for k in range(1, owners):
            gather_copy(s, k).wait()

        def load(step, col):
            return gathered[s, :, pl.ds(col, 128)]

        def store(step, col, value):
            source[:, pl.ds(col, KA)] = value.astype(f32)

        whiten_rows(load, store, tables, turned.at[0 : 9 * group, :], spec.at[0 : 9 * group, :])

        @pl.loop(0, TB)
        def _(q):
            col_re = pl.ds(pl.multiple_of(q * 2 * KA, KA), KA)
            col_im = pl.ds(pl.multiple_of(q * 2 * KA + KA, KA), KA)
            rows = [[pl.ds(w * held + n, 1) for w in range(windows)] for n in range(held)]
            wave = [[(source[r, col_re], source[r, col_im]) for r in line] for line in rows]
            wave = [
                [tuple(jnp.broadcast_to(v, (16, KA)) for v in (x, y, x - y)) for x, y in line]
                for line in wave
            ]
            for g in range(block // 16):
                at = [pl.ds(w * block + g * 16, 16) for w in range(windows)]
                a = [own[r, col_re] for r in at]
                b = [own[r, col_im] for r in at]
                c = [x + y for x, y in zip(a, b)]
                for n in range(held):
                    sums = []
                    for factor, which in ((a, 0), (b, 1), (c, 2)):
                        total = factor[0] * wave[n][0][which]
                        for w in range(1, windows):
                            total = total + factor[w] * wave[n][w][which]
                        sums.append(total)
                    to = pl.ds(n * block + g * 16, 16)
                    cross[to, col_re] = (sums[0] + sums[1]).astype(bf16)
                    cross[to, col_im] = (sums[2] - sums[0] + sums[1]).astype(bf16)

        out = jnp.dot(cross[...], inv_ref[...], preferred_element_type=f32) * scale
        out = out.astype(bf16)
        for j in range(ends):
            end = chunk_of(s) * ends + j
            part[end] = out[j * per * block : (j + 1) * per * block]
            k = lax.rem(end - time + shards, shards)

            @pl.when(k != 0)
            def _():
                remote(part.at[end], parts.at[k], send_a.at[k], recv_a.at[k], "tm", end).start()

    def by_source(k):
        return remote(part.at[times[k]], parts.at[k], send_a.at[k], recv_a.at[k], "tm", times[k])

    def by_owner(p, k):
        src, dst = leaving.at[p, chans[k]], arrived.at[p, chan]
        return remote(src, dst, send_b.at[p, k], recv_b.at[p, k], "chan", chans[k])

    def by_row(p, k):
        rows = pl.ds(pl.multiple_of(times[k] * share, share), share)
        src, dst = placed.at[p, rows, :], final.at[p, time]
        return remote(src, dst, send_c.at[p, k], recv_c.at[p, k], "tm", times[k])

    for k in range(1, shards):
        by_source(k).wait()
    each = per // PIECES
    for p in range(PIECES):
        for n in range(each):
            rows = pl.ds((p * each + n) * block, block)
            total = part[time, rows, :].astype(f32)
            for k in range(1, shards):
                total = total + parts[k, rows, :].astype(f32)
            totals[p, :, pl.ds(n * LAGS, LAGS)] = total.astype(bf16)
        if slots % 16 == 0:
            value = jnp.dot(send_ref[...].astype(bf16), totals[p], preferred_element_type=f32)
            leaving[p] = value.astype(bf16).reshape(owners, slots, wide)
        else:
            for o in range(owners):
                mask = send_ref[pl.ds(o * slots, slots), :].astype(bf16)
                leaving[p, o] = jnp.dot(mask, totals[p], preferred_element_type=f32).astype(bf16)
        for k in range(1, owners):
            by_owner(p, k).start()
        arrived[p, chan] = leaving[p, chan]

    for p in range(PIECES):
        for k in range(1, owners):
            by_owner(p, k).wait()
        if slots % 16 == 0:
            stacked = arrived[p].reshape(owners * slots, wide)
        else:
            stacked = jnp.concatenate([arrived[p, o].astype(f32) for o in range(owners)], axis=0).astype(bf16)
        placed[p] = jnp.dot(take_ref[...], stacked, preferred_element_type=f32).astype(bf16)
        for k in range(1, shards):
            by_row(p, k).start()
        final[p, time] = placed[p, pl.ds(pl.multiple_of(time * share, share), share), :]
    for p in range(PIECES):
        for k in range(1, shards):
            by_row(p, k).wait()
        for m in range(shards):
            for n in range(each):
                value = final[p, m, :, pl.ds(n * LAGS, LAGS)].astype(f32)
                out_ref[:, m * per + p * each + n, :] = value


def run(traces, lists, source_owner, source_slot, shards, owners, windows, scale, tables):
    capacity = lists.shape[1]
    block = traces.shape[0] // windows
    group = 16
    held = group // windows
    sources = source_slot.size
    chunks = sources // held
    assert chunks == windows and held % (sources // shards) == 0
    slots = (capacity + owners - 1) // owners
    share = capacity // shards
    smem = pl.BlockSpec(memory_space=pltpu.SMEM)
    per = sources // shards
    wide = per // PIECES * LAGS
    most = max(block, group)
    vmem = pl.BlockSpec(memory_space=pltpu.VMEM)
    bf16, f32 = jnp.bfloat16, jnp.float32
    sems = lambda *shape: [pltpu.SemaphoreType.DMA(shape)] * 2
    return pl.pallas_call(
        functools.partial(kernel, owners, shards, block, windows, scale, slots),
        in_specs=[vmem] * 2 + [smem] * 3 + [vmem] * 5 + [pl.BlockSpec(memory_space=pl.ANY)],
        out_specs=vmem,
        out_shape=jax.ShapeDtypeStruct((share, sources, LAGS), f32),
        scratch_shapes=[
            pltpu.VMEM((chunks, group, L), bf16),
            pltpu.VMEM((owners * slots, block), f32),
            pltpu.VMEM((capacity, owners * slots), bf16),
            pltpu.VMEM((9 * most, 2 * TA), bf16),
            pltpu.VMEM((9 * most, 4 * KA), f32),
            pltpu.VMEM((windows * block, L), f32),
            pltpu.VMEM((group, L), f32),
            pltpu.VMEM((held * block, L), bf16),
            pltpu.VMEM((L, LAGS), bf16),
            pltpu.VMEM((chunks, owners, group, L // owners), bf16),
            pltpu.VMEM((chunks, group, L // owners), bf16),
            pltpu.VMEM((chunks, group, L), bf16),
            pltpu.VMEM((shards, per * block, LAGS), bf16),
            pltpu.VMEM((shards, per * block, LAGS), bf16),
            pltpu.VMEM((PIECES, block, wide), bf16),
            pltpu.VMEM((PIECES, owners, slots, wide), bf16),
            pltpu.VMEM((PIECES, owners, slots, wide), bf16),
            pltpu.VMEM((PIECES, capacity, wide), bf16),
            pltpu.VMEM((PIECES, shards, share, wide), bf16),
            pltpu.SemaphoreType.DMA,
        ]
        + sems(chunks, owners) + sems(chunks, owners)
        + sems(shards) + sems(PIECES, owners) + sems(PIECES, shards),
        compiler_params=pltpu.CompilerParams(collective_id=0, has_side_effects=True),
        name="correlations",
    )(traces, lists, lists, source_owner, source_slot, *tables)


def body(raw_traces, owner_lists, source_owner, source_slot):
    block, windows, length = raw_traces.shape
    owners, shards = lax.axis_size("chan"), lax.axis_size("tm")
    tables = tuple(jnp.asarray(t) for t in make_tables())
    scale = 1.0 / math.sqrt(windows * shards * HALF)
    traces = jnp.transpose(raw_traces, (1, 0, 2)).reshape(windows * block, length)
    return run(
        traces, owner_lists, source_owner, source_slot, shards, owners, windows, scale, tables
    )


def solution(mesh):
    return jax.shard_map(
        body,
        mesh=mesh,
        in_specs=(P("chan", "tm", None), P(), P(), P()),
        out_specs=P(("chan", "tm"), None, None),
        check_vma=False,
    )
```

```python
import functools
import math

import jax
import jax.numpy as jnp
import numpy as np
from jax import lax
from jax.experimental import pallas as pl
from jax.experimental.pallas import tpu as pltpu
from jax.sharding import PartitionSpec as P

L = 4096
HALF = L // 2
HW = 64
LAGS = 256
EPSILON = 1e-06
TB = 16
TA = L // TB
KA = HALF // TB


def make_tables():
    a = np.arange(TA, dtype=np.int64)
    taper = 0.5 - 0.5 * np.cos(2 * np.pi / L * (np.arange(L) + 0.5))
    kb = np.arange(TB // 2 + 1, dtype=np.int64)
    twist = 2 * np.pi / L * (kb[:, None] * a[None, :])
    twist_cos, twist_sin = np.cos(twist), np.sin(twist)
    ka = np.arange(KA, dtype=np.int64)
    low = 2 * np.pi / TA * (a[:, None] * ka[None, :] % TA)
    high = 2 * np.pi / TA * (a[:, None] * (TA - 1 - ka)[None, :] % TA)
    top = [np.cos(low), -np.sin(low), np.cos(high), np.sin(high)]
    bottom = [np.sin(low), np.cos(low), np.sin(high), -np.cos(high)]
    second = np.concatenate([np.concatenate(top, 1), np.concatenate(bottom, 1)], 0)
    bins = np.arange(TB)[:, None] + TB * ka[None, :]
    counts = np.minimum(bins, HW) + np.minimum(HALF - 1 - bins, HW) + 1
    lag = np.arange(LAGS, dtype=np.int64) - LAGS // 2
    angle = 2 * np.pi / L * (bins[:, :, None] * lag % L)
    weight = np.where(bins == 0, 1.0, 2.0)[:, :, None]
    inverse = np.stack([weight * np.cos(angle), -weight * np.sin(angle)], 1)
    f32 = np.float32
    return (
        taper.astype(f32)[None, :],
        twist_cos.astype(f32),
        twist_sin.astype(f32),
        second.astype(jnp.bfloat16),
        (1.0 / counts).astype(f32),
        inverse.reshape(L, LAGS).astype(jnp.bfloat16),
    )


def dft4(x0, x1, x2, x3):
    if x0[1] is None:
        s, d = x0[0] + x2[0], x0[0] - x2[0]
        u, v = x1[0] + x3[0], x1[0] - x3[0]
        return (s + u, None), (d, -v), (s - u, None), (d, v)
    sr, si, dr, di = x0[0] + x2[0], x0[1] + x2[1], x0[0] - x2[0], x0[1] - x2[1]
    ur, ui, vr, vi = x1[0] + x3[0], x1[1] + x3[1], x1[0] - x3[0], x1[1] - x3[1]
    return (sr + ur, si + ui), (dr + vi, di - vr), (sr - ur, si - ui), (dr - vi, di + vr)


def turn(value, step):
    c, s = math.cos(2 * math.pi * step / TB), math.sin(2 * math.pi * step / TB)
    re, im = value
    if step == 0:
        return value
    if im is None:
        return re * c, re * (-s)
    return re * c + im * s, im * c - re * s


def dft16_real(x):
    first = [dft4(*[(x[n + 4 * m], None) for m in range(4)]) for n in range(4)]
    out = [None] * 9
    for q in range(3):
        parts = [turn(first[n][q], n * q) for n in range(4)]
        if q == 0:
            r = [p[0] for p in parts]
            out[0] = (r[0] + r[1] + r[2] + r[3], None)
            out[4] = (r[0] - r[2], r[3] - r[1])
            out[8] = ((r[0] + r[2]) - (r[1] + r[3]), None)
        else:
            if parts[0][1] is None:
                parts[0] = (parts[0][0], jnp.zeros_like(parts[0][0]))
            y = dft4(*parts)
            out[q] = y[0]
            out[q + 4] = y[1]
            if q == 1:
                out[3] = (y[3][0], -y[3][1])
            else:
                pass
    parts = [turn(first[n][1], n) for n in range(4)]
    y = dft4(*parts)
    out[7] = (y[2][0], -y[2][1])
    return out


def whiten_rows(load, store, tables, turned, spec):
    taper_ref, cos_ref, sin_ref, second_ref, count_ref = tables
    rows = turned.shape[0] // 9
    place = {q: (q - 1) * rows for q in range(1, 9)}
    place[0] = 8 * rows
    group = 16

    @pl.loop(0, rows // group)
    def _(step):
        base = pl.multiple_of(step * group, group)
        for h in range(TA // 128):
            x = []
            for b in range(TB):
                cols = pl.ds(b * TA + h * 128, 128)
                v = load(step, b * TA + h * 128).astype(jnp.float32) * taper_ref[:, cols]
                x.append(v.astype(jnp.bfloat16).astype(jnp.float32))
            y = dft16_real(x)
            here = pl.ds(h * 128, 128)
            there = pl.ds(TA + h * 128, 128)
            for q in range(TB // 2 + 1):
                re, im = y[q]
                target = pl.ds(pl.multiple_of(base + place[q], group), group)
                if q == 0:
                    out_re, out_im = re, jnp.zeros_like(re)
                else:
                    c, s = cos_ref[pl.ds(q, 1), here], sin_ref[pl.ds(q, 1), here]
                    if im is None:
                        out_re, out_im = re * c, -(re * s)
                    else:
                        out_re, out_im = re * c + im * s, im * c - re * s
                turned[target, here] = out_re.astype(jnp.bfloat16)
                turned[target, there] = out_im.astype(jnp.bfloat16)

    split = 7 * rows
    spec[0:split, :] = jnp.dot(
        turned[0:split, :], second_ref[...], preferred_element_type=jnp.float32
    )
    spec[split:, 0 : 2 * KA] = jnp.dot(
        turned[split:, :], second_ref[:, 0 : 2 * KA], preferred_element_type=jnp.float32
    )

    lane = lax.broadcasted_iota(jnp.int32, (8, KA), 1)

    def ahead(v, d):
        return jnp.where(lane < KA - d, pltpu.roll(v, KA - d, 1), 0.0)

    def behind(v, d):
        return jnp.where(lane >= d, pltpu.roll(v, d, 1), 0.0)

    @pl.loop(0, rows // 16)
    def _(step):
        done = [[], []]
        for half in range(2):
            base = pl.multiple_of(step * 16, 16) + half * 8

            def part(q, imag):
                src, col = (q, 0) if q <= 8 else (TB - q, 2 * KA)
                at = pl.ds(pl.multiple_of(base + place[src], 8), 8)
                return spec[at, pl.ds(col + imag * KA, KA)]

            mags = []
            for q in range(TB):
                re, im = part(q, 0), part(q, 1)
                m = jnp.sqrt(re * re + im * im)
                mags.append(m.astype(jnp.bfloat16).astype(jnp.float32))
            prefix = [mags[0]]
            for q in range(1, TB):
                prefix.append(prefix[-1] + mags[q])
            total = prefix[-1]
            near = total
            for d in (1, 2, 3):
                near = near + ahead(total, d) + behind(total, d)
            suffix = total
            for q in range(TB):
                smooth = near + behind(suffix, 4) + ahead(prefix[q], 4)
                suffix = suffix - mags[q]
                inv = 1.0 / (smooth * count_ref[pl.ds(q, 1), :] + EPSILON)
                done[half].append((part(q, 0) * inv, part(q, 1) * inv))
        for q in range(TB):
            for p in range(2):
                both = jnp.concatenate([done[0][q][p], done[1][q][p]], axis=0)
                store(step, q * 2 * KA + p * KA, both.astype(jnp.bfloat16))


def partners(axis, extent):
    me = lax.axis_index(axis)
    return me, [lax.rem(me + k, extent) for k in range(extent)]


def remote(src, dst, send, recv, axis, device):
    return pltpu.make_async_remote_copy(
        src_ref=src,
        dst_ref=dst,
        send_sem=send,
        recv_sem=recv,
        device_id={axis: device},
        device_id_type=pl.DeviceIdType.MESH,
    )


def greet(pairs):
    barrier = pltpu.get_barrier_semaphore()
    for axis, device in pairs:
        pl.semaphore_signal(
            barrier, inc=1, device_id={axis: device}, device_id_type=pl.DeviceIdType.MESH
        )
    return lambda: pl.semaphore_wait(barrier, len(pairs))


PIECES = 2


def kernel(
    owners, shards, block, windows, scale,
    slots, traces_ref, lists_ref, lists_s, owner_s, slot_s, taper_ref, cos_ref, sin_ref, second_ref, count_ref, inv_hbm,
    out_ref,
    mine_ref, send_ref, take_ref, turned, spec, own, source, cross, inv_ref, shares, piece, gathered, part, parts, totals,
    leaving, arrived, placed, final,
    inv_sem, send_r, recv_r, send_g, recv_g, send_a, recv_a, send_b, recv_b, send_c, recv_c,
):
    tables = (taper_ref, cos_ref, sin_ref, second_ref, count_ref)
    f32, bf16 = jnp.float32, jnp.bfloat16
    chunks, group, _ = mine_ref.shape
    held = group // windows
    width = L // owners
    per = part.shape[1] // block
    ends = held // per
    share = out_ref.shape[0]
    wide = totals.shape[2]
    chan, chans = partners("chan", owners)
    time, times = partners("tm", shards)
    home = time // ends
    pairs = [("chan", chans[k]) for k in range(1, owners)] + [("tm", times[k]) for k in range(1, shards)]
    all_here = greet(pairs)

    def iota(shape, dim):
        return lax.broadcasted_iota(jnp.int32, shape, dim)

    shape = (chunks * group, windows * block)
    row, col = iota(shape, 0), iota(shape, 1)
    which = row // group * held + row % held
    wanted = jnp.full(shape, -1, jnp.int32)
    steps, each_step = slot_s.shape
    for i in range(steps * each_step):
        channel = lists_s[owner_s[i // each_step], slot_s[i // each_step, i % each_step]]
        wanted = jnp.where(which == i, channel, wanted)
    hit = (wanted == chan * block + col % block) & (col // block == row // held % windows)
    pick = jnp.where(hit, 1.0, 0.0).astype(bf16)

    @pl.loop(0, L // 1024)
    def _(t):
        at = pl.ds(pl.multiple_of(t * 1024, 1024), 1024)
        rows = jnp.dot(pick, traces_ref[:, at], preferred_element_type=f32).astype(bf16)
        for g in range(chunks):
            mine_ref[g, :, at] = rows[g * group : (g + 1) * group]

    all_here()

    def cut(device):
        return pl.ds(pl.multiple_of(device * width, 128), width)

    def chunk_of(s):
        return lax.rem(home + 1 + s, chunks)

    def reduce_copy(s, k):
        src = mine_ref.at[chunk_of(s), :, cut(chans[k])]
        return remote(src, shares.at[s, k], send_r.at[s, k], recv_r.at[s, k], "chan", chans[k])

    def gather_copy(s, k):
        dst = gathered.at[s, :, cut(chan)]
        return remote(piece.at[s], dst, send_g.at[s, k], recv_g.at[s, k], "chan", chans[k])

    for s in range(2):
        for k in range(1, owners):
            reduce_copy(s, k).start()
    inv_copy = pltpu.make_async_copy(inv_hbm, inv_ref, inv_sem)
    inv_copy.start()

    capacity = lists_ref.shape[1]
    before = jnp.where(iota((capacity, capacity), 0) <= iota((capacity, capacity), 1), 1.0, 0.0)
    lists = lists_ref[...]
    here = (lists >= chan * block) & (lists < (chan + 1) * block)
    inside = jnp.where(here, lists - chan * block, -1).astype(f32)
    wall = (owners * slots, capacity)
    spread = jnp.where(
        iota((owners * slots, owners), 0) // slots == iota((owners * slots, owners), 1), 1.0, 0.0
    )
    offset = jnp.dot(spread, inside, preferred_element_type=f32)
    live = offset >= 0
    slot = (iota(wall, 0) % slots + 1).astype(f32)
    rank = jnp.dot(jnp.where(live, 1.0, 0.0), before, preferred_element_type=f32)
    channel = jnp.sum(jnp.where(live & (rank == slot), offset + 1.0, 0.0), axis=1, keepdims=True) - 1.0
    send_ref[...] = jnp.where(
        channel == iota((owners * slots, block), 1).astype(f32), 1.0, 0.0
    )
    listed = jnp.broadcast_to(lists_ref[pl.ds(chan, 1), :], wall)
    start = iota(wall, 0) // slots * block
    found = (listed >= start) & (listed < start + block)
    rank = jnp.dot(jnp.where(found, 1.0, 0.0), before, preferred_element_type=f32)
    take = jnp.where(found & (rank == slot), 1.0, 0.0)
    take_ref[...] = take.T.astype(bf16)

    @pl.loop(0, windows)
    def _(w):
        def load(step, col):
            at = pl.ds(pl.multiple_of(w * block + step * group, group), group)
            return traces_ref[at, pl.ds(col, 128)]

        def store(step, col, value):
            at = pl.ds(pl.multiple_of(w * block + step * group, group), group)
            own[at, pl.ds(col, KA)] = value.astype(f32)

        whiten_rows(load, store, tables, turned, spec)

        total = mine_ref[chunk_of(w), :, cut(chan)].astype(f32)
        for k in range(1, owners):
            reduce_copy(w, k).wait()
            total = total + shares[w, k].astype(f32)
        piece[w] = total.astype(bf16)
        gathered[w, :, cut(chan)] = total.astype(bf16)
        for k in range(1, owners):
            gather_copy(w, k).start()

        @pl.when(w + 2 < chunks)
        def _():
            for k in range(1, owners):
                reduce_copy(w + 2, k).start()

    inv_copy.wait()

    @pl.loop(0, chunks)
    def _(s):
        for k in range(1, owners):
            gather_copy(s, k).wait()

        def load(step, col):
            return gathered[s, :, pl.ds(col, 128)]

        def store(step, col, value):
            source[:, pl.ds(col, KA)] = value.astype(f32)

        whiten_rows(load, store, tables, turned.at[0 : 9 * group, :], spec.at[0 : 9 * group, :])

        @pl.loop(0, TB)
        def _(q):
            col_re = pl.ds(pl.multiple_of(q * 2 * KA, KA), KA)
            col_im = pl.ds(pl.multiple_of(q * 2 * KA + KA, KA), KA)
            rows = [[pl.ds(w * held + n, 1) for w in range(windows)] for n in range(held)]
            wave = [[(source[r, col_re], source[r, col_im]) for r in line] for line in rows]
            wave = [
                [tuple(jnp.broadcast_to(v, (16, KA)) for v in (x, y, x - y)) for x, y in line]
                for line in wave
            ]
            for g in range(block // 16):
                at = [pl.ds(w * block + g * 16, 16) for w in range(windows)]
                a = [own[r, col_re] for r in at]
                b = [own[r, col_im] for r in at]
                c = [x + y for x, y in zip(a, b)]
                for n in range(held):
                    sums = []
                    for factor, which in ((a, 0), (b, 1), (c, 2)):
                        total = factor[0] * wave[n][0][which]
                        for w in range(1, windows):
                            total = total + factor[w] * wave[n][w][which]
                        sums.append(total)
                    to = pl.ds(n * block + g * 16, 16)
                    cross[to, col_re] = (sums[0] + sums[1]).astype(bf16)
                    cross[to, col_im] = (sums[2] - sums[0] + sums[1]).astype(bf16)

        out = jnp.dot(cross[...], inv_ref[...], preferred_element_type=f32) * scale
        out = out.astype(bf16)
        for j in range(ends):
            end = chunk_of(s) * ends + j
            part[end] = out[j * per * block : (j + 1) * per * block]
            k = lax.rem(end - time + shards, shards)

            @pl.when(k != 0)
            def _():
                remote(part.at[end], parts.at[k], send_a.at[k], recv_a.at[k], "tm", end).start()

    def by_source(k):
        return remote(part.at[times[k]], parts.at[k], send_a.at[k], recv_a.at[k], "tm", times[k])

    def by_owner(p, k):
        src, dst = leaving.at[p, chans[k]], arrived.at[p, chan]
        return remote(src, dst, send_b.at[p, k], recv_b.at[p, k], "chan", chans[k])

    def by_row(p, k):
        rows = pl.ds(pl.multiple_of(times[k] * share, share), share)
        src, dst = placed.at[p, rows, :], final.at[p, time]
        return remote(src, dst, send_c.at[p, k], recv_c.at[p, k], "tm", times[k])

    for k in range(1, shards):
        by_source(k).wait()
    each = per // PIECES
    for p in range(PIECES):
        for n in range(each):
            rows = pl.ds((p * each + n) * block, block)
            total = part[time, rows, :].astype(f32)
            for k in range(1, shards):
                total = total + parts[k, rows, :].astype(f32)
            totals[p, :, pl.ds(n * LAGS, LAGS)] = total.astype(bf16)
        if slots % 16 == 0:
            value = jnp.dot(send_ref[...].astype(bf16), totals[p], preferred_element_type=f32)
            leaving[p] = value.astype(bf16).reshape(owners, slots, wide)
        else:
            for o in range(owners):
                mask = send_ref[pl.ds(o * slots, slots), :].astype(bf16)
                leaving[p, o] = jnp.dot(mask, totals[p], preferred_element_type=f32).astype(bf16)
        for k in range(1, owners):
            by_owner(p, k).start()
        arrived[p, chan] = leaving[p, chan]

    for p in range(PIECES):
        for k in range(1, owners):
            by_owner(p, k).wait()
        if slots % 16 == 0:
            stacked = arrived[p].reshape(owners * slots, wide)
        else:
            stacked = jnp.concatenate([arrived[p, o].astype(f32) for o in range(owners)], axis=0).astype(bf16)
        placed[p] = jnp.dot(take_ref[...], stacked, preferred_element_type=f32).astype(bf16)
        for k in range(1, shards):
            by_row(p, k).start()
        final[p, time] = placed[p, pl.ds(pl.multiple_of(time * share, share), share), :]
    for p in range(PIECES):
        for k in range(1, shards):
            by_row(p, k).wait()
        for m in range(shards):
            for n in range(each):
                value = final[p, m, :, pl.ds(n * LAGS, LAGS)].astype(f32)
                out_ref[:, m * per + p * each + n, :] = value


def run(traces, lists, source_owner, source_slot, shards, owners, windows, scale, tables):
    capacity = lists.shape[1]
    block = traces.shape[0] // windows
    group = 16
    held = group // windows
    sources = source_slot.size
    chunks = sources // held
    assert chunks == windows and held % (sources // shards) == 0
    slots = (capacity + owners - 1) // owners
    share = capacity // shards
    smem = pl.BlockSpec(memory_space=pltpu.SMEM)
    per = sources // shards
    wide = per // PIECES * LAGS
    most = max(block, group)
    vmem = pl.BlockSpec(memory_space=pltpu.VMEM)
    bf16, f32 = jnp.bfloat16, jnp.float32
    sems = lambda *shape: [pltpu.SemaphoreType.DMA(shape)] * 2
    return pl.pallas_call(
        functools.partial(kernel, owners, shards, block, windows, scale, slots),
        in_specs=[vmem] * 2 + [smem] * 3 + [vmem] * 5 + [pl.BlockSpec(memory_space=pl.ANY)],
        out_specs=vmem,
        out_shape=jax.ShapeDtypeStruct((share, sources, LAGS), f32),
        scratch_shapes=[
            pltpu.VMEM((chunks, group, L), bf16),
            pltpu.VMEM((owners * slots, block), f32),
            pltpu.VMEM((capacity, owners * slots), bf16),
            pltpu.VMEM((9 * most, 2 * TA), bf16),
            pltpu.VMEM((9 * most, 4 * KA), f32),
            pltpu.VMEM((windows * block, L), f32),
            pltpu.VMEM((group, L), f32),
            pltpu.VMEM((held * block, L), bf16),
            pltpu.VMEM((L, LAGS), bf16),
            pltpu.VMEM((chunks, owners, group, L // owners), bf16),
            pltpu.VMEM((chunks, group, L // owners), bf16),
            pltpu.VMEM((chunks, group, L), bf16),
            pltpu.VMEM((shards, per * block, LAGS), bf16),
            pltpu.VMEM((shards, per * block, LAGS), bf16),
            pltpu.VMEM((PIECES, block, wide), bf16),
            pltpu.VMEM((PIECES, owners, slots, wide), bf16),
            pltpu.VMEM((PIECES, owners, slots, wide), bf16),
            pltpu.VMEM((PIECES, capacity, wide), bf16),
            pltpu.VMEM((PIECES, shards, share, wide), bf16),
            pltpu.SemaphoreType.DMA,
        ]
        + sems(chunks, owners) + sems(chunks, owners)
        + sems(shards) + sems(PIECES, owners) + sems(PIECES, shards),
        compiler_params=pltpu.CompilerParams(collective_id=0, has_side_effects=True, vmem_limit_bytes=32 << 20),
        name="correlations",
    )(traces, lists, lists, source_owner, source_slot, *tables)


def body(raw_traces, owner_lists, source_owner, source_slot):
    block, windows, length = raw_traces.shape
    owners, shards = lax.axis_size("chan"), lax.axis_size("tm")
    tables = tuple(jnp.asarray(t) for t in make_tables())
    scale = 1.0 / math.sqrt(windows * shards * HALF)
    traces = jnp.transpose(raw_traces, (1, 0, 2)).reshape(windows * block, length)
    return run(
        traces, owner_lists, source_owner, source_slot, shards, owners, windows, scale, tables
    )


def solution(mesh):
    return jax.shard_map(
        body,
        mesh=mesh,
        in_specs=(P("chan", "tm", None), P(), P(), P()),
        out_specs=P(("chan", "tm"), None, None),
        check_vma=False,
    )
```
